512 devices in a mesh: grp: 16 (over z_hi, x, core), shard: 32 (over y, z_lo).
Axes of the slice: x: 4, y: 8, z: 8 (z_hi: 2, z_lo: 4; z = z_hi * 4 + z_lo), core: 2. Of those that a mesh axis runs over, the one named last changes fastest.
Arguments:
- query_states: bfloat16 [131072, 512], P(('grp', 'shard')), may hold values from -7.5 to 7.5
- key_states: bfloat16 [131072, 512], P(('grp', 'shard')), may hold values from -7.5 to 7.5
- value_states: bfloat16 [131072, 512], P(('grp', 'shard')), may hold values from -7.5 to 7.5
- valid_mask: int32 [131072], P(('grp', 'shard')), may hold values from 0 to 1, as said below
- attended_grad: bfloat16 [131072, 512], P(('grp', 'shard')), may hold values from -7.5 to 7.5
Outputs:
- attended: bfloat16 [131072, 512], P(('grp', 'shard'))
- query_grad: bfloat16 [131072, 512], P(('grp', 'shard'))
- key_grad: bfloat16 [131072, 512], P(('grp', 'shard'))
- value_grad: bfloat16 [131072, 512], P(('grp', 'shard'))
The draws below stay inside these ranges and needn't reach their ends.
Inputs may be any that keep to these rules, and one draw needn't show every extreme that they name: `valid_mask`: in each device's run of 256 positions the ones form a prefix of 64 to 256 positions; the first run is all ones and the last has exactly 64.
All inputs are finite; a program needn't handle non-finite values.
Results may differ from the reference program's by a relative error of at most 0.0055.
Values may be sent and summed in bfloat16 or wider, within the bound.
No kernel may reach another device: no remote copies, remote signals or barrier semaphores. Data moves between devices by JAX's collectives and lax.ppermute only.
A program may use at most 128 MiB of HBM per device.

```python
import jax
import jax.numpy as jnp
from jax import lax

HEADS = 4
HEAD_DIM = 128
WIDTH = 512
BLOCK = 128
COARSE = 64
TOK_DEV = 256
LEVELS = 9
TOKENS = 131072


LIMIT = 7.5


def session_table(key, amp):
    seg_len = max(TOKENS // (4 * COARSE), 1)
    table = jax.random.normal(key, (TOKENS // seg_len, WIDTH), jnp.float32) * amp
    return jnp.repeat(table, seg_len, axis=0)


def draw_query_states(key, part):
    rough = jnp.clip(jax.random.normal(jax.random.fold_in(key, 11), (TOKENS, WIDTH), jnp.float32), -LIMIT, LIMIT)
    return rough.astype(jnp.bfloat16)


def draw_key_states(key, part):
    rough = 0.8 * jax.random.normal(jax.random.fold_in(key, 21), (TOKENS, WIDTH), jnp.float32) + session_table(jax.random.fold_in(key, 22), 0.6)
    rough = jnp.clip(rough, -LIMIT, LIMIT)
    return rough.astype(jnp.bfloat16)


def draw_value_states(key, part):
    rough = 0.8 * jax.random.normal(jax.random.fold_in(key, 31), (TOKENS, WIDTH), jnp.float32) + session_table(jax.random.fold_in(key, 32), 0.6)
    return jnp.clip(rough, -LIMIT, LIMIT).astype(jnp.bfloat16)


def draw_attended_grad(key, part):
    common = jax.random.normal(jax.random.fold_in(key, 45), (1, WIDTH), jnp.float32)
    rough = 0.7 * jax.random.normal(jax.random.fold_in(key, 41), (TOKENS, WIDTH), jnp.float32)
    rough = rough + session_table(jax.random.fold_in(key, 44), 0.5) + 0.5 * common
    return jnp.clip(rough, -LIMIT, LIMIT).astype(jnp.bfloat16)


def draw_valid_mask(key, part):
    device_count = TOKENS // TOK_DEV
    lengths = jax.random.randint(jax.random.fold_in(key, 51), (device_count,), TOK_DEV // 4, TOK_DEV + 1)
    lengths = lengths.at[0].set(TOK_DEV).at[device_count - 1].set(TOK_DEV // 4)
    positions = jnp.arange(TOK_DEV, dtype=jnp.int32)
    return (positions[None, :] < lengths[:, None]).astype(jnp.int32).reshape(TOKENS)


def setup_inputs(seed: int = 0) -> dict:
    seeds = jax.random.split(jax.random.key(seed), 6)
    query_states = draw_query_states(jax.random.fold_in(seeds[5], 71), 0)
    key_states = draw_key_states(jax.random.fold_in(seeds[5], 71), 0)
    value_states = draw_value_states(jax.random.fold_in(seeds[5], 71), 0)
    valid_mask = draw_valid_mask(jax.random.fold_in(seeds[5], 71), 0)
    attended_grad = draw_attended_grad(jax.random.fold_in(seeds[5], 71), 0)
    return dict(query_states=query_states, key_states=key_states, value_states=value_states, valid_mask=valid_mask, attended_grad=attended_grad)


MASKED = -1.0e30


def flip_pairs(array):
    shape = array.shape
    paired = array.reshape((shape[0] // 2, 2) + shape[1:])
    return jnp.flip(paired, axis=1).reshape(shape)


def reference(query_states, key_states, value_states, valid_mask, attended_grad):
    feat_width = query_states.shape[1]
    score_scale = HEAD_DIM ** -0.5
    mask_float = valid_mask.astype(jnp.float32)
    kv_states = jnp.stack([key_states, value_states], axis=1)
    sib_means = []
    sib_live = []
    count_tables = []
    for lvl in range(LEVELS):
        group_size = (BLOCK * 2 ** (lvl + 1)) // COARSE
        row_count = TOKENS // group_size
        group_sums = jnp.sum(kv_states.reshape(row_count, group_size, 2, feat_width).astype(jnp.float32) * mask_float.reshape(row_count, group_size, 1, 1), axis=1)
        group_count = jnp.sum(mask_float.reshape(row_count, group_size), axis=1)
        group_means = (group_sums / jnp.maximum(group_count, 1.0)[:, None, None]).astype(jnp.bfloat16)
        span_count = row_count // COARSE
        sib_means.append(flip_pairs(group_means.reshape(span_count, COARSE, 2, feat_width)))
        sib_live.append(flip_pairs(group_count.reshape(span_count, COARSE)) > 0)
        count_tables.append(group_count.reshape(span_count, COARSE))
    span_len = 2 * BLOCK
    nspans = TOKENS // span_len
    far_rows = LEVELS * COARSE
    padded_kv = jnp.pad(kv_states, ((BLOCK, BLOCK), (0, 0), (0, 0)))
    padded_mask = jnp.pad(mask_float, (BLOCK, BLOCK))
    near_init = jnp.zeros((TOKENS + 2 * BLOCK, 2, feat_width), jnp.float32)
    grad_init = tuple(jnp.zeros(table.shape, jnp.float32) for table in sib_means)

    def step(state_carry, span_index):
        near_acc, grad_acc = state_carry
        row_start = span_index * span_len
        query_span = lax.dynamic_slice_in_dim(query_states, row_start, span_len, 0).astype(jnp.float32).reshape(2, BLOCK, HEADS, HEAD_DIM)
        cot_span = lax.dynamic_slice_in_dim(attended_grad, row_start, span_len, 0).astype(jnp.float32).reshape(2, BLOCK, HEADS, HEAD_DIM)
        window = lax.dynamic_slice_in_dim(padded_kv, row_start, 4 * BLOCK, 0)
        window_mask = lax.dynamic_slice_in_dim(padded_mask, row_start, 4 * BLOCK, 0)
        near_kv = jnp.stack([window[:3 * BLOCK], window[BLOCK:]], axis=0).astype(jnp.float32)
        near_mask = jnp.stack([window_mask[:3 * BLOCK], window_mask[BLOCK:]], axis=0)
        near_keys = near_kv[:, :, 0].reshape(2, 3 * BLOCK, HEADS, HEAD_DIM)
        near_vals = near_kv[:, :, 1].reshape(2, 3 * BLOCK, HEADS, HEAD_DIM)
        far_kv = jnp.concatenate([lax.dynamic_index_in_dim(sib_means[lvl], span_index // (2 ** lvl), 0, keepdims=False) for lvl in range(LEVELS)], axis=0).astype(jnp.float32)
        far_ok = jnp.concatenate([lax.dynamic_index_in_dim(sib_live[lvl], span_index // (2 ** lvl), 0, keepdims=False) for lvl in range(LEVELS)], axis=0)
        far_keys = far_kv[:, 0].reshape(far_rows, HEADS, HEAD_DIM)
        far_vals = far_kv[:, 1].reshape(far_rows, HEADS, HEAD_DIM)
        near_score = jnp.einsum("bqhd,bkhd->bqhk", query_span, near_keys) * score_scale
        near_score = jnp.where(near_mask[:, None, None, :] > 0, near_score, MASKED)
        far_score = jnp.einsum("bqhd,khd->bqhk", query_span, far_keys) * score_scale
        far_score = jnp.where(far_ok[None, None, None, :], far_score, MASKED)
        row_max = jnp.maximum(jnp.max(near_score, axis=-1), jnp.max(far_score, axis=-1))
        near_exp = jnp.exp(near_score - row_max[..., None])
        far_exp = jnp.exp(far_score - row_max[..., None])
        row_total = jnp.sum(near_exp, axis=-1) + jnp.sum(far_exp, axis=-1)
        near_prob = near_exp / row_total[..., None]
        far_prob = far_exp / row_total[..., None]
        nearby_half_rows = lax.optimization_barrier(near_prob.astype(jnp.bfloat16)).astype(jnp.float32)
        far_half = lax.optimization_barrier(far_prob.astype(jnp.bfloat16)).astype(jnp.float32)
        attended_span = jnp.einsum("bqhk,bkhd->bqhd", nearby_half_rows, near_vals) + jnp.einsum("bqhk,khd->bqhd", far_half, far_vals)
        near_dp = jnp.einsum("bqhd,bkhd->bqhk", cot_span, near_vals)
        far_dp = jnp.einsum("bqhd,khd->bqhk", cot_span, far_vals)
        row_delta = jnp.sum(near_prob * near_dp, axis=-1) + jnp.sum(far_prob * far_dp, axis=-1)
        nearby_delta_score = lax.optimization_barrier((near_prob * (near_dp - row_delta[..., None])).astype(jnp.bfloat16)).astype(jnp.float32)
        far_ds = lax.optimization_barrier((far_prob * (far_dp - row_delta[..., None])).astype(jnp.bfloat16)).astype(jnp.float32)
        query_span_grad = score_scale * (jnp.einsum("bqhk,bkhd->bqhd", nearby_delta_score, near_keys) + jnp.einsum("bqhk,khd->bqhd", far_ds, far_keys))
        near_gk = score_scale * jnp.einsum("bqhk,bqhd->bkhd", nearby_delta_score, query_span)
        near_gv = jnp.einsum("bqhk,bqhd->bkhd", nearby_half_rows, cot_span)
        near_grad = jnp.stack([near_gk.reshape(2, 3 * BLOCK, feat_width), near_gv.reshape(2, 3 * BLOCK, feat_width)], axis=2)
        window_grad = jnp.zeros((4 * BLOCK, 2, feat_width), jnp.float32)
        window_grad = window_grad.at[:3 * BLOCK].add(near_grad[0]).at[BLOCK:].add(near_grad[1])
        old_rows = lax.dynamic_slice_in_dim(near_acc, row_start, 4 * BLOCK, 0)
        near_acc = lax.dynamic_update_slice_in_dim(near_acc, old_rows + window_grad, row_start, 0)
        far_gk = score_scale * jnp.einsum("bqhk,bqhd->khd", far_ds, query_span)
        far_gv = jnp.einsum("bqhk,bqhd->khd", far_half, cot_span)
        far_grad = jnp.stack([far_gk.reshape(far_rows, feat_width), far_gv.reshape(far_rows, feat_width)], axis=1)
        new_acc = []
        for lvl in range(LEVELS):
            position = span_index // (2 ** lvl)
            piece = far_grad[lvl * COARSE:(lvl + 1) * COARSE]
            old_tile = lax.dynamic_index_in_dim(grad_acc[lvl], position, 0, keepdims=False)
            new_acc.append(lax.dynamic_update_index_in_dim(grad_acc[lvl], old_tile + piece, position, 0))
        outputs = (attended_span.reshape(span_len, feat_width).astype(jnp.bfloat16), query_span_grad.reshape(span_len, feat_width).astype(jnp.bfloat16))
        return (near_acc, tuple(new_acc)), outputs

    final_carry, stacked = lax.scan(step, (near_init, grad_init), jnp.arange(nspans, dtype=jnp.int32))
    near_acc, grad_acc = final_carry
    attended = stacked[0].reshape(TOKENS, feat_width)
    query_grad = stacked[1].reshape(TOKENS, feat_width)
    kv_grad = near_acc[BLOCK:BLOCK + TOKENS]
    for lvl in range(LEVELS):
        group_size = (BLOCK * 2 ** (lvl + 1)) // COARSE
        row_count = TOKENS // group_size
        tile_grad = flip_pairs(grad_acc[lvl]) / jnp.maximum(count_tables[lvl], 1.0)[..., None, None]
        spread = tile_grad.reshape(row_count, 1, 2, feat_width) * mask_float.reshape(row_count, group_size, 1, 1)
        kv_grad = kv_grad + spread.reshape(TOKENS, 2, feat_width)
    return attended, query_grad, kv_grad[:, 0].astype(jnp.bfloat16), kv_grad[:, 1].astype(jnp.bfloat16)
```

```python
import jax
import jax.numpy as jnp
from jax import lax
from jax.experimental import pallas as pl
from jax.experimental.pallas import tpu as pltpu
from jax.sharding import PartitionSpec as P

HEADS = 4
HEAD_DIM = 128
BLOCK = 128
COARSE = 64
LEVELS = 9
LANES = 128
MASKED = -1e30
VMEM_BYTES = 56 * 1024 * 1024

f32 = jnp.float32
bf16 = jnp.bfloat16


def rows_of(shape):
    return lax.broadcasted_iota(jnp.int32, shape, 0)


def call(kernel, outs, scratch, index, *operands, flops=0, name=None):
    size = sum(o.size * o.dtype.itemsize for o in operands)
    size += sum(o.size * o.dtype.itemsize for o in outs)
    in_specs = [pl.BlockSpec(memory_space=pltpu.SMEM)]
    in_specs += [pl.BlockSpec(memory_space=pltpu.VMEM) for _ in operands]
    return pl.pallas_call(
        kernel,
        out_shape=outs,
        in_specs=in_specs,
        out_specs=[pl.BlockSpec(memory_space=pltpu.VMEM) for _ in outs],
        scratch_shapes=scratch,
        compiler_params=pltpu.CompilerParams(vmem_limit_bytes=VMEM_BYTES),
        cost_estimate=pl.CostEstimate(flops=flops, bytes_accessed=size, transcendentals=0),
        name=name,
    )(index, *operands)


def shape(rows, width, dtype=bf16):
    return jax.ShapeDtypeStruct((rows, width), dtype)


def by_lanes(column, width):
    return jnp.concatenate([column] * (width // LANES), axis=1)


def decode_count(code):
    lane = lax.broadcasted_iota(jnp.int32, code.shape, 1)
    part = jnp.where(lane < LANES // 2, 8.0 * code, code)
    return part + pltpu.roll(part, LANES // 2, 1)


def encode_count(count):
    lane = lax.broadcasted_iota(jnp.int32, count.shape, 1)
    high = jnp.floor(count * 0.125)
    return jnp.where(lane < LANES // 2, high, count - 8.0 * high)


def local_kernel(width, peers):
    def kernel(index, mask, key, value, sib, oth, gather):
        parity = index[0]
        tokens = key.shape[0]
        length = jnp.sum(mask[...], axis=1, keepdims=True)
        live = (rows_of((tokens, LANES)) < length).astype(bf16)
        for ref, block in ((sib, 1 - parity), (oth, parity)):
            start = pl.multiple_of(block * BLOCK, BLOCK)
            ref[pl.ds(0, BLOCK), pl.ds(0, width)] = key[pl.ds(start, BLOCK)]
            ref[pl.ds(0, BLOCK), pl.ds(width, width)] = value[pl.ds(start, BLOCK)]
            place = rows_of((BLOCK, LANES)) + start
            ref[pl.ds(0, BLOCK), pl.ds(2 * width, LANES)] = (place < length).astype(f32).astype(bf16)

        def means(rows):
            group = tokens // rows
            row = rows_of((rows, tokens))
            place = lax.broadcasted_iota(jnp.int32, (rows, tokens), 1)
            member = (row * group <= place) & (place < row * group + group) & (place < length)
            member = member.astype(f32).astype(bf16)
            first = rows_of((rows, LANES)) * group
            count = jnp.clip(length - first, 0, group).astype(f32)
            inverse = by_lanes(1.0 / jnp.maximum(count, 1.0), width)
            k_sum = jnp.dot(member, key[...], preferred_element_type=f32)
            v_sum = jnp.dot(member, value[...], preferred_element_type=f32)
            return (k_sum * inverse).astype(bf16), (v_sum * inverse).astype(bf16), count.astype(bf16)

        k_mean, v_mean, count = means(COARSE)
        sib[pl.ds(BLOCK, COARSE), pl.ds(0, width)] = k_mean
        sib[pl.ds(BLOCK, COARSE), pl.ds(width, width)] = v_mean
        sib[pl.ds(BLOCK, COARSE), pl.ds(2 * width, LANES)] = count
        few = gather.shape[1]
        k_mean, v_mean, count = means(few)
        for peer in range(peers):
            gather[peer, :, pl.ds(0, width)] = k_mean
            gather[peer, :, pl.ds(width, width)] = v_mean
            gather[peer, :, pl.ds(2 * width, LANES)] = count

    return kernel


def store_means(out, first, sums, count, scale_width):
    inverse = by_lanes(1.0 / jnp.maximum(count, 1.0), scale_width)
    rows = count.shape[0]
    out[pl.ds(first, rows), pl.ds(0, scale_width)] = (sums * inverse).astype(bf16)
    out[pl.ds(first, rows), pl.ds(scale_width, LANES)] = count.astype(bf16)


def load_sums(ref, first, rows, sums, counts, at, coded=False):
    width = sums.shape[0] * LANES
    count = ref[pl.ds(first, rows), pl.ds(width, LANES)].astype(f32)
    if coded:
        count = decode_count(count)
    counts[pl.ds(at, rows)] = count
    for tile in range(sums.shape[0]):
        mean = ref[pl.ds(first, rows), pl.ds(tile * LANES, LANES)].astype(f32)
        sums[tile, pl.ds(at, rows)] = mean * count


def climb_kernel(first_own, first_other, bit):
    def kernel(index, own, other, out, sums, counts):
        side = index[bit]
        at_own = pl.multiple_of(side * COARSE, COARSE)
        at_other = pl.multiple_of((1 - side) * COARSE, COARSE)
        load_sums(own, first_own, COARSE, sums, counts, at_own)
        load_sums(other, first_other, COARSE, sums, counts, at_other)
        store_means(
            out, 0, pooled(sums, COARSE, 2), pooled(counts, COARSE, 2), sums.shape[0] * LANES
        )

    return kernel


def pooled(ref, rows, step):
    if len(ref.shape) == 3:
        return jnp.concatenate(
            [pooled(ref.at[tile], rows, step) for tile in range(ref.shape[0])], axis=1
        )
    total = ref[pl.ds(0, rows, stride=step)]
    for i in range(1, step):
        total = total + ref[pl.ds(i, rows, stride=step)]
    return total


def group_kernel(groups):
    def kernel(index, recv, six, seven, wide, sums, counts):
        width = sums.shape[0] * LANES
        total = recv.shape[0]
        load_sums(recv, 0, total, sums, counts, 0)
        quarter = total // COARSE
        store_means(six, 0, pooled(sums, COARSE, quarter), pooled(counts, COARSE, quarter), width)
        half = COARSE // 2
        store_means(
            seven, 0, pooled(sums, half, 2 * quarter), pooled(counts, half, 2 * quarter), width
        )
        few = wide.shape[1]
        step = total // few
        count = pooled(counts, few, step)
        inverse = by_lanes(1.0 / jnp.maximum(count, 1.0), width)
        mean = (pooled(sums, few, step) * inverse).astype(bf16)
        code = encode_count(count).astype(bf16)
        for peer in range(groups):
            wide[peer, :, pl.ds(0, width)] = mean
            wide[peer, :, pl.ds(width, LANES)] = code

    return kernel


def attention_kernel(width, shard_rows, group_rows):
    far_rows = LEVELS * COARSE
    scale = HEAD_DIM**-0.5
    main_rows = far_rows + 2 * BLOCK
    key_rows = main_rows + BLOCK
    half = COARSE // 2

    def kernel(
        index, query, cot, sib, oth, sib_in, oth_in, two_in, three_in, shard_in, six_in,
        seven_a, seven_b, group_in,
        attended, query_grad, own_grad, sib_grad, oth_grad, low_grad, three_out,
        shard_part, six_out, seven_a_out, seven_b_out, group_out,
        keys, bias, inverse, sums, counts, score, weight, grads,
    ):
        parity, octet, half_shard, quad_group, half_group = (
            index[0], index[4], index[5], index[6], index[7]
        )
        packed = 2 * width

        def take(at, ref, first, rows):
            keys[pl.ds(at, rows)] = ref[pl.ds(first, rows), pl.ds(0, packed)]
            count = ref[pl.ds(first, rows), pl.ds(packed, LANES)].astype(f32)
            bias[pl.ds(at, rows)] = jnp.where(count > 0, 0.0, MASKED)
            if at < far_rows:
                inverse[pl.ds(at, rows)] = 1.0 / jnp.maximum(count, 1.0)

        def take_pooled(at):
            count = pooled(counts, COARSE, 2)
            inv = 1.0 / jnp.maximum(count, 1.0)
            keys[pl.ds(at, COARSE)] = (pooled(sums, COARSE, 2) * by_lanes(inv, packed)).astype(bf16)
            bias[pl.ds(at, COARSE)] = jnp.where(count > 0, 0.0, MASKED)
            inverse[pl.ds(at, COARSE)] = inv

        octet_at = pl.multiple_of(octet * COARSE, COARSE)
        half_shard_at = pl.multiple_of(half_shard * 2 * COARSE, 2 * COARSE)
        quad_at = pl.multiple_of(quad_group * COARSE, COARSE)
        half_group_at = pl.multiple_of(half_group * 2 * COARSE, 2 * COARSE)
        take(0, sib_in, BLOCK, COARSE)
        take(COARSE, two_in, 0, COARSE)
        take(2 * COARSE, three_in, 0, COARSE)
        take(3 * COARSE, shard_in, octet_at, COARSE)
        load_sums(shard_in, half_shard_at, 2 * COARSE, sums, counts, 0)
        take_pooled(4 * COARSE)
        take(5 * COARSE, six_in, 0, COARSE)
        take(6 * COARSE, seven_a, 0, half)
        take(6 * COARSE + half, seven_b, 0, half)
        at = 7 * COARSE
        keys[pl.ds(at, COARSE)] = group_in[pl.ds(quad_at, COARSE), pl.ds(0, packed)]
        count = decode_count(group_in[pl.ds(quad_at, COARSE), pl.ds(packed, LANES)].astype(f32))
        bias[pl.ds(at, COARSE)] = jnp.where(count > 0, 0.0, MASKED)
        inverse[pl.ds(at, COARSE)] = 1.0 / jnp.maximum(count, 1.0)
        load_sums(group_in, half_group_at, 2 * COARSE, sums, counts, 0, coded=True)
        take_pooled(8 * COARSE)
        take(far_rows, sib, 0, BLOCK)
        take(far_rows + BLOCK, oth, 0, BLOCK)
        take(main_rows, sib_in, 0, BLOCK)
        take(main_rows + BLOCK, oth_in, 0, BLOCK)

        own_rows = (
            pl.ds(pl.multiple_of((1 - parity) * BLOCK, BLOCK), BLOCK),
            pl.ds(pl.multiple_of(parity * BLOCK, BLOCK), BLOCK),
        )
        nt = (((1,), (1,)), ((), ()))
        tn = (((0,), (0,)), ((), ()))
        segments = [(at, 64) for at in range(0, main_rows, 64)]
        halo_segments = [(at, 64) for at in range(0, BLOCK, 64)]

        def one_head(head):
            key_cols = pl.ds(pl.multiple_of(head * HEAD_DIM, HEAD_DIM), HEAD_DIM)
            value_cols = pl.ds(pl.multiple_of(width + head * HEAD_DIM, HEAD_DIM), HEAD_DIM)
            q = jnp.concatenate([query[r, key_cols] for r in own_rows], axis=0)
            c = jnp.concatenate([cot[r, key_cols] for r in own_rows], axis=0)

            def dots(cols, side):
                return (
                    lax.dot_general(keys[pl.ds(0, main_rows), cols], side, nt, preferred_element_type=f32),
                    lax.dot_general(
                        keys[pl.ds(main_rows, BLOCK), cols], side[:BLOCK], nt, preferred_element_type=f32
                    ),
                    lax.dot_general(
                        keys[pl.ds(main_rows + BLOCK, BLOCK), cols], side[BLOCK:], nt,
                        preferred_element_type=f32,
                    ),
                )

            main, near_sib, near_oth = dots(key_cols, q)
            score[pl.ds(0, main_rows)] = main * scale + by_lanes(bias[pl.ds(0, main_rows)], 2 * BLOCK)
            score[pl.ds(main_rows, BLOCK)] = jnp.concatenate(
                [
                    near_sib * scale + bias[pl.ds(main_rows, BLOCK)],
                    near_oth * scale + bias[pl.ds(main_rows + BLOCK, BLOCK)],
                ],
                axis=1,
            )
            main, near_sib, near_oth = dots(value_cols, c)
            grads[pl.ds(0, main_rows)] = main
            grads[pl.ds(main_rows, BLOCK)] = jnp.concatenate([near_sib, near_oth], axis=1)
            top = jnp.full((8, 2 * BLOCK), -jnp.inf, f32)
            for at in range(0, key_rows, 64):
                part = score[pl.ds(at, 64)]
                top = jnp.maximum(top, jnp.max(part.reshape(8, 8, 2 * BLOCK), axis=0))
            top = jnp.max(top, axis=0, keepdims=True)
            total = jnp.zeros((8, 2 * BLOCK), f32)
            mixed = jnp.zeros((8, 2 * BLOCK), f32)
            for at in range(0, key_rows, 64):
                e = jnp.exp(score[pl.ds(at, 64)] - top)
                score[pl.ds(at, 64)] = e
                total = total + jnp.sum(e.reshape(8, 8, 2 * BLOCK), axis=0)
                mixed = mixed + jnp.sum((e * grads[pl.ds(at, 64)]).reshape(8, 8, 2 * BLOCK), axis=0)
            total = 1.0 / jnp.sum(total, axis=0, keepdims=True)
            delta = jnp.sum(mixed, axis=0, keepdims=True) * total
            for at in range(0, key_rows, 64):
                prob = score[pl.ds(at, 64)] * total
                weight[pl.ds(at, 64), pl.ds(0, 2 * BLOCK)] = prob.astype(bf16)
                ds = prob * (grads[pl.ds(at, 64)] - delta)
                weight[pl.ds(at, 64), pl.ds(2 * BLOCK, 2 * BLOCK)] = ds.astype(bf16)

            def back(offset, cols):
                out = lax.dot_general(
                    weight[pl.ds(0, main_rows), pl.ds(offset, 2 * BLOCK)],
                    keys[pl.ds(0, main_rows), cols], tn, preferred_element_type=f32,
                )
                near = []
                for i in range(2):
                    near.append(
                        lax.dot_general(
                            weight[pl.ds(main_rows, BLOCK), pl.ds(offset + i * BLOCK, BLOCK)],
                            keys[pl.ds(main_rows + i * BLOCK, BLOCK), cols], tn,
                            preferred_element_type=f32,
                        )
                    )
                return out + jnp.concatenate(near, axis=0)

            out = back(0, value_cols)
            grad = back(2 * BLOCK, key_cols) * scale
            for i, r in enumerate(own_rows):
                attended[r, key_cols] = out[i * BLOCK : (i + 1) * BLOCK].astype(bf16)
                query_grad[r, key_cols] = grad[i * BLOCK : (i + 1) * BLOCK].astype(bf16)

            for offset, cols, side, factor in (
                (2 * BLOCK, key_cols, q, scale), (0, value_cols, c, None)
            ):
                res = jnp.dot(
                    weight[pl.ds(0, main_rows), pl.ds(offset, 2 * BLOCK)], side,
                    preferred_element_type=f32,
                )
                if factor is not None:
                    res = res * factor
                far = res[:far_rows] * inverse[...]
                own_grad[:, cols] = res[far_rows:]
                low_grad[:, cols] = far[: 2 * COARSE]
                three_out[:, cols] = far[2 * COARSE : 3 * COARSE].astype(bf16)
                shard_part[pl.ds(0, 2 * COARSE), cols] = far[3 * COARSE : 5 * COARSE]
                six_out[:, cols] = far[5 * COARSE : 6 * COARSE].astype(bf16)
                seven_a_out[:, cols] = far[6 * COARSE : 6 * COARSE + half].astype(bf16)
                seven_b_out[:, cols] = far[6 * COARSE + half : 7 * COARSE].astype(bf16)
                sums[head + (0 if offset else HEADS)] = far[7 * COARSE :]
                for i, out_ref in enumerate((sib_grad, oth_grad)):
                    near = jnp.dot(
                        weight[pl.ds(main_rows, BLOCK), pl.ds(offset + i * BLOCK, BLOCK)],
                        side[i * BLOCK : (i + 1) * BLOCK], preferred_element_type=f32,
                    )
                    if factor is not None:
                        near = near * factor
                    out_ref[:, cols] = near.astype(bf16)

        def step(head, carry):
            one_head(head)
            return carry

        lax.fori_loop(0, HEADS, step, 0)
        group_out[...] = jnp.zeros_like(group_out)
        for tile in range(sums.shape[0]):
            cols = pl.ds(tile * LANES, LANES)
            group_out[pl.ds(quad_at, COARSE), cols] = sums[tile, pl.ds(0, COARSE)].astype(bf16)
            wide = widen(sums[tile, pl.ds(COARSE, COARSE)], 2)
            group_out[pl.ds(half_group_at, 2 * COARSE), cols] = wide.astype(bf16)

    scratch = [
        pltpu.VMEM((key_rows + BLOCK, 2 * width), bf16),
        pltpu.VMEM((key_rows + BLOCK, LANES), f32),
        pltpu.VMEM((far_rows, LANES), f32),
        pltpu.VMEM((2 * width // LANES, 2 * COARSE, LANES), f32),
        pltpu.VMEM((2 * COARSE, LANES), f32),
        pltpu.VMEM((key_rows, 2 * BLOCK), f32),
        pltpu.VMEM((key_rows, 4 * BLOCK), bf16),
        pltpu.VMEM((key_rows, 2 * BLOCK), f32),
    ]
    outs = [
        shape(2 * BLOCK, width), shape(2 * BLOCK, width), shape(2 * BLOCK, 2 * width, f32),
        shape(BLOCK, 2 * width), shape(BLOCK, 2 * width), shape(2 * COARSE, 2 * width, f32),
        shape(COARSE, 2 * width), shape(2 * COARSE, 2 * width, f32), shape(COARSE, 2 * width),
        shape(half, 2 * width), shape(half, 2 * width), shape(group_rows, 2 * width),
    ]
    return kernel, outs, scratch


def widen(rows, times):
    count, width = rows.shape
    return jnp.broadcast_to(rows[:, None], (count, times, width)).reshape(count * times, width)


def shard_back_kernel(index, part, six, seven_a, seven_b, group, out, acc):
    octet, half_shard = index[4], index[5]
    tile = six[...].astype(f32) + widen(seven_a[...].astype(f32) + seven_b[...].astype(f32), 2)
    few = COARSE // 4
    total = group[pl.ds(0, few)].astype(f32)
    for i in range(1, group.shape[0] // few):
        total = total + group[pl.ds(i * few, few)].astype(f32)
    tile = tile + widen(total, 4)
    acc[...] = widen(tile, out.shape[0] // COARSE)
    octet_at = pl.ds(pl.multiple_of(octet * COARSE, COARSE), COARSE)
    half_at = pl.ds(pl.multiple_of(half_shard * 2 * COARSE, 2 * COARSE), 2 * COARSE)
    acc[octet_at] = acc[octet_at] + part[pl.ds(0, COARSE)]
    acc[half_at] = acc[half_at] + widen(part[pl.ds(COARSE, COARSE)], 2)
    out[...] = acc[...].astype(bf16)


def two_back_kernel(index, three, low, out):
    side = index[1]
    half = COARSE // 2
    theirs = three[pl.ds(pl.multiple_of((1 - side) * half, half), half)].astype(f32)
    out[...] = (low[pl.ds(COARSE, COARSE)] + widen(theirs, 2)).astype(bf16)


def one_back_kernel(index, three, two, low, sib_grad, out, mine, tile):
    side, low_side = index[1], index[0]
    half = COARSE // 2
    upper = three[pl.ds(pl.multiple_of(side * half, half), half)].astype(f32)
    tile[...] = widen(upper, 2) + two[...].astype(f32)
    theirs = tile[pl.ds(pl.multiple_of((1 - low_side) * half, half), half)]
    out[pl.ds(0, BLOCK)] = sib_grad[...]
    out[pl.ds(BLOCK, COARSE)] = (low[pl.ds(0, COARSE)] + widen(theirs, 2)).astype(bf16)
    mine[...] = tile[pl.ds(pl.multiple_of(low_side * half, half), half)]


def final_kernel(width):
    def kernel(index, mask, own, sib_back, oth_back, mine, shard, key_grad, value_grad, spread):
        parity = index[0]
        tokens = key_grad.shape[0]
        length = jnp.sum(mask[...], axis=1, keepdims=True)
        few = shard.shape[1]
        total = shard[0].astype(f32)
        for i in range(1, shard.shape[0]):
            total = total + shard[i].astype(f32)
        tile = widen(total, COARSE // few) + widen(mine[...], 2)
        tile = tile + sib_back[pl.ds(BLOCK, COARSE)].astype(f32)
        spread[...] = widen(tile, tokens // COARSE)
        for i, (block, near) in enumerate(((1 - parity, sib_back), (parity, oth_back))):
            start = pl.multiple_of(block * BLOCK, BLOCK)
            live = (rows_of((BLOCK, LANES)) + start < length).astype(f32)
            grad = own[pl.ds(i * BLOCK, BLOCK)] + near[pl.ds(0, BLOCK)].astype(f32)
            grad = grad + spread[pl.ds(start, BLOCK)] * by_lanes(live, 2 * width)
            key_grad[pl.ds(start, BLOCK)] = grad[:, :width].astype(bf16)
            value_grad[pl.ds(start, BLOCK)] = grad[:, width:].astype(bf16)

    return kernel


def flip(count, bits):
    return [(i, i ^ bits) for i in range(count)]


def body(query_states, key_states, value_states, valid_mask, attended_grad):
    tokens, width = query_states.shape
    shards = lax.axis_size("shard")
    groups = lax.axis_size("grp")
    total = shards * groups
    packed = 2 * width
    row = packed + LANES
    half = COARSE // 2
    s = lax.axis_index("shard")
    g = lax.axis_index("grp")
    index = jnp.stack(
        [s & 1, s >> 1 & 1, s >> 2 & 1, s, s >> 3 ^ 1, s >> 4 ^ 1, g >> 2 ^ 1, g >> 3 ^ 1]
    ).astype(jnp.int32)
    mask = valid_mask.reshape(1, tokens)
    pairs = [(2 * i - 1, 2 * i) for i in range(1, total // 2)]
    pairs = pairs + [(high, low) for low, high in pairs]

    def on_shard(x, bits):
        return lax.ppermute(x, "shard", flip(shards, bits))

    def on_group(x, bits):
        return lax.ppermute(x, "grp", flip(groups, bits))

    few_shard = 2 * COARSE // 16
    few_group = COARSE // 4
    sib, oth, gather = call(
        local_kernel(width, shards),
        [
            shape(BLOCK + COARSE, row), shape(BLOCK, row),
            jax.ShapeDtypeStruct((shards, few_shard, row), bf16),
        ],
        [], index, mask, key_states, value_states, name="local",
    )
    sib_in = on_shard(sib, 1)
    oth_in = lax.ppermute(oth, ("grp", "shard"), pairs)
    shard_in = lax.all_to_all(gather, "shard", 0, 0, tiled=True).reshape(shards * few_shard, row)
    tile_scratch = [
        pltpu.VMEM((packed // LANES, 2 * COARSE, LANES), f32),
        pltpu.VMEM((2 * COARSE, LANES), f32),
    ]
    (two,) = call(
        climb_kernel(BLOCK, BLOCK, 0), [shape(COARSE, row)], tile_scratch, index, sib, sib_in, name="climb_two"
    )
    two_in = on_shard(two, 2)
    six, seven, wide = call(
        group_kernel(groups),
        [shape(COARSE, row), shape(half, row), jax.ShapeDtypeStruct((groups, few_group, row), bf16)],
        [
            pltpu.VMEM((packed // LANES, shards * few_shard, LANES), f32),
            pltpu.VMEM((shards * few_shard, LANES), f32),
        ],
        index, shard_in, name="climb_six",
    )
    six_in = on_group(six, 1)
    seven_a = on_group(seven, 2)
    seven_b = on_group(seven, 3)
    group_in = lax.all_to_all(wide, "grp", 0, 0, tiled=True).reshape(groups * few_group, row)
    (three,) = call(
        climb_kernel(0, 0, 1), [shape(COARSE, row)], tile_scratch, index, two, two_in, name="climb_three"
    )
    three_in = on_shard(three, 4)
    kernel, outs, scratch = attention_kernel(width, shards * few_shard, groups * few_group)
    (
        attended, query_grad, own_grad, sib_grad, oth_grad, low_grad, three_out, shard_part,
        six_out, seven_a_out, seven_b_out, group_out,
    ) = call(
        kernel, outs, scratch, index, query_states, attended_grad, sib, oth, sib_in, oth_in,
        two_in, three_in, shard_in, six_in, seven_a, seven_b, group_in,
        flops=1_600_000_000, name="attention",
    )
    six_back = on_group(six_out, 1)
    seven_a_back = on_group(seven_a_out, 2)
    seven_b_back = on_group(seven_b_out, 3)
    three_back = on_shard(three_out, 4)
    oth_back = lax.ppermute(oth_grad, ("grp", "shard"), pairs)
    group_back = lax.all_to_all(group_out, "grp", 0, 0, tiled=True)
    (two_out,) = call(
        two_back_kernel, [shape(COARSE, packed)], [], index, three_back, low_grad, name="back_two"
    )
    two_back = on_shard(two_out, 2)
    (shard_out,) = call(
        shard_back_kernel, [shape(shards * few_shard, packed)],
        [pltpu.VMEM((shards * few_shard, packed), f32)],
        index, shard_part, six_back, seven_a_back, seven_b_back, group_back, name="back_six",
    )
    sib_out, mine = call(
        one_back_kernel, [shape(BLOCK + COARSE, packed), shape(half, packed, f32)],
        [pltpu.VMEM((COARSE, packed), f32)],
        index, three_back, two_back, low_grad, sib_grad, name="back_one",
    )
    sib_back = on_shard(sib_out, 1)
    shard_back = lax.all_to_all(shard_out, "shard", 0, 0, tiled=True)
    key_grad, value_grad = call(
        final_kernel(width), [shape(tokens, width), shape(tokens, width)],
        [pltpu.VMEM((tokens, packed), f32)],
        index, mask, own_grad, sib_back, oth_back, mine,
        shard_back.reshape(shards, few_shard, packed), name="final",
    )
    return attended, query_grad, key_grad, value_grad


def solution(mesh):
    whole = P(("grp", "shard"), None)
    return jax.shard_map(
        body,
        mesh=mesh,
        in_specs=(whole, whole, whole, P(("grp", "shard")), whole),
        out_specs=(whole, whole, whole, whole),
        check_vma=False,
    )
```

```python
import jax
import jax.numpy as jnp
from jax import lax
from jax.experimental import pallas as pl
from jax.experimental.pallas import tpu as pltpu
from jax.sharding import PartitionSpec as P

HEADS = 4
HEAD_DIM = 128
BLOCK = 128
COARSE = 64
LEVELS = 9
LANES = 128
MASKED = -1e30
VMEM_BYTES = 56 * 1024 * 1024

f32 = jnp.float32
bf16 = jnp.bfloat16


def rows_of(shape):
    return lax.broadcasted_iota(jnp.int32, shape, 0)


def call(kernel, outs, scratch, index, *operands, flops=0, name=None):
    size = sum(o.size * o.dtype.itemsize for o in operands)
    size += sum(o.size * o.dtype.itemsize for o in outs)
    in_specs = [pl.BlockSpec(memory_space=pltpu.SMEM)]
    in_specs += [pl.BlockSpec(memory_space=pltpu.VMEM) for _ in operands]
    return pl.pallas_call(
        kernel,
        out_shape=outs,
        in_specs=in_specs,
        out_specs=[pl.BlockSpec(memory_space=pltpu.VMEM) for _ in outs],
        scratch_shapes=scratch,
        compiler_params=pltpu.CompilerParams(vmem_limit_bytes=VMEM_BYTES),
        cost_estimate=pl.CostEstimate(flops=flops, bytes_accessed=size, transcendentals=0),
        name=name,
    )(index, *operands)


def shape(rows, width, dtype=bf16):
    return jax.ShapeDtypeStruct((rows, width), dtype)


def by_lanes(column, width):
    return jnp.concatenate([column] * (width // LANES), axis=1)


def decode_count(code):
    lane = lax.broadcasted_iota(jnp.int32, code.shape, 1)
    part = jnp.where(lane < LANES // 2, 8.0 * code, code)
    return part + pltpu.roll(part, LANES // 2, 1)


def encode_count(count):
    lane = lax.broadcasted_iota(jnp.int32, count.shape, 1)
    high = jnp.floor(count * 0.125)
    return jnp.where(lane < LANES // 2, high, count - 8.0 * high)


def local_kernel(width, peers):
    def kernel(index, mask, key, value, sib, oth, pair, gather):
        parity = index[0]
        tokens = key.shape[0]
        length = jnp.sum(mask[...], axis=1, keepdims=True)
        for ref, block in ((sib, 1 - parity), (oth, parity)):
            start = pl.multiple_of(block * BLOCK, BLOCK)
            ref[pl.ds(0, BLOCK), pl.ds(0, width)] = key[pl.ds(start, BLOCK)]
            ref[pl.ds(0, BLOCK), pl.ds(width, width)] = value[pl.ds(start, BLOCK)]
            place = rows_of((BLOCK, LANES)) + start
            ref[pl.ds(0, BLOCK), pl.ds(2 * width, LANES)] = (place < length).astype(f32).astype(bf16)

        def means(rows):
            group = tokens // rows
            row = rows_of((rows, tokens))
            place = lax.broadcasted_iota(jnp.int32, (rows, tokens), 1)
            member = (row * group <= place) & (place < row * group + group) & (place < length)
            member = member.astype(f32).astype(bf16)
            first = rows_of((rows, LANES)) * group
            count = jnp.clip(length - first, 0, group).astype(f32)
            inverse = by_lanes(1.0 / jnp.maximum(count, 1.0), width)
            k_sum = jnp.dot(member, key[...], preferred_element_type=f32)
            v_sum = jnp.dot(member, value[...], preferred_element_type=f32)
            return (k_sum * inverse).astype(bf16), (v_sum * inverse).astype(bf16), count.astype(bf16)

        k_mean, v_mean, count = means(COARSE)
        sib[pl.ds(BLOCK, COARSE), pl.ds(0, width)] = k_mean
        sib[pl.ds(BLOCK, COARSE), pl.ds(width, width)] = v_mean
        sib[pl.ds(BLOCK, COARSE), pl.ds(2 * width, LANES)] = count
        k_mean, v_mean, count = means(COARSE // 2)
        pair[:, pl.ds(0, width)] = k_mean
        pair[:, pl.ds(width, width)] = v_mean
        pair[:, pl.ds(2 * width, LANES)] = count
        few = gather.shape[1]
        k_mean, v_mean, count = means(few)
        for peer in range(peers):
            gather[peer, :, pl.ds(0, width)] = k_mean
            gather[peer, :, pl.ds(width, width)] = v_mean
            gather[peer, :, pl.ds(2 * width, LANES)] = count

    return kernel


def store_means(out, first, sums, count, scale_width):
    inverse = by_lanes(1.0 / jnp.maximum(count, 1.0), scale_width)
    rows = count.shape[0]
    out[pl.ds(first, rows), pl.ds(0, scale_width)] = (sums * inverse).astype(bf16)
    out[pl.ds(first, rows), pl.ds(scale_width, LANES)] = count.astype(bf16)


def load_sums(ref, first, rows, sums, counts, at, coded=False):
    width = sums.shape[0] * LANES
    count = ref[pl.ds(first, rows), pl.ds(width, LANES)].astype(f32)
    if coded:
        count = decode_count(count)
    counts[pl.ds(at, rows)] = count
    for tile in range(sums.shape[0]):
        mean = ref[pl.ds(first, rows), pl.ds(tile * LANES, LANES)].astype(f32)
        sums[tile, pl.ds(at, rows)] = mean * count


def pooled(ref, rows, step, base=0):
    if len(ref.shape) == 3:
        return jnp.concatenate(
            [pooled(ref.at[tile], rows, step, base) for tile in range(ref.shape[0])], axis=1
        )
    total = ref[pl.ds(base, rows, stride=step)]
    for i in range(1, step):
        total = total + ref[pl.ds(base + i, rows, stride=step)]
    return total


def quarter_at(index, flip_bits):
    few = COARSE // 4
    return pl.multiple_of(((index[3] & 3) ^ flip_bits) * few, few)


def climb_kernel(groups):
    def kernel(
        index, sib_in, pair, pair_a, pair_b, recv, three, six, seven, wide, sums, counts
    ):
        width = sums.shape[0] * LANES
        total = recv.shape[0]
        load_sums(recv, 0, total, sums, counts, 0)
        quarter = total // COARSE
        store_means(six, 0, pooled(sums, COARSE, quarter), pooled(counts, COARSE, quarter), width)
        half = COARSE // 2
        store_means(
            seven, 0, pooled(sums, half, 2 * quarter), pooled(counts, half, 2 * quarter), width
        )
        few = wide.shape[1]
        step = total // few
        count = pooled(counts, few, step)
        inverse = by_lanes(1.0 / jnp.maximum(count, 1.0), width)
        mean = (pooled(sums, few, step) * inverse).astype(bf16)
        code = encode_count(count).astype(bf16)
        for peer in range(groups):
            wide[peer, :, pl.ds(0, width)] = mean
            wide[peer, :, pl.ds(width, LANES)] = code
        few = COARSE // 4
        for ref, first, rows, bits in (
            (pair, 0, half, 0), (sib_in, BLOCK, COARSE, 1), (pair_a, 0, half, 2), (pair_b, 0, half, 3)
        ):
            base = bits * COARSE
            load_sums(ref, first, rows, sums, counts, base)
            step = rows // few
            store_means(
                three, quarter_at(index, bits), pooled(sums, few, step, base),
                pooled(counts, few, step, base), width,
            )

    return kernel


def attention_kernel(width, shard_rows, group_rows):
    far_rows = LEVELS * COARSE
    scale = HEAD_DIM**-0.5
    main_rows = far_rows + 2 * BLOCK
    key_rows = main_rows + BLOCK
    half = COARSE // 2

    def kernel(
        index, query, cot, sib, oth, sib_in, oth_in, pair_a, pair_b, three_in, shard_in, six_in,
        seven_a, seven_b, group_in,
        attended, query_grad, own_grad, sib_grad, oth_grad, low_grad, three_out,
        shard_part, six_out, seven_a_out, seven_b_out, group_out,
        keys, bias, inverse, sums, counts, score, weight, grads,
    ):
        parity, octet, half_shard, quad_group, half_group = (
            index[0], index[4], index[5], index[6], index[7]
        )
        packed = 2 * width

        def take(at, ref, first, rows):
            keys[pl.ds(at, rows)] = ref[pl.ds(first, rows), pl.ds(0, packed)]
            count = ref[pl.ds(first, rows), pl.ds(packed, LANES)].astype(f32)
            bias[pl.ds(at, rows)] = jnp.where(count > 0, 0.0, MASKED)
            if at < far_rows:
                inverse[pl.ds(at, rows)] = 1.0 / jnp.maximum(count, 1.0)

        def take_pooled(at):
            count = pooled(counts, COARSE, 2)
            inv = 1.0 / jnp.maximum(count, 1.0)
            keys[pl.ds(at, COARSE)] = (pooled(sums, COARSE, 2) * by_lanes(inv, packed)).astype(bf16)
            bias[pl.ds(at, COARSE)] = jnp.where(count > 0, 0.0, MASKED)
            inverse[pl.ds(at, COARSE)] = inv

        octet_at = pl.multiple_of(octet * COARSE, COARSE)
        half_shard_at = pl.multiple_of(half_shard * 2 * COARSE, 2 * COARSE)
        quad_at = pl.multiple_of(quad_group * COARSE, COARSE)
        half_group_at = pl.multiple_of(half_group * 2 * COARSE, 2 * COARSE)
        take(0, sib_in, BLOCK, COARSE)
        take(COARSE, pair_a, 0, half)
        take(COARSE + half, pair_b, 0, half)
        take(2 * COARSE, three_in, 0, COARSE)
        take(3 * COARSE, shard_in, octet_at, COARSE)
        load_sums(shard_in, half_shard_at, 2 * COARSE, sums, counts, 0)
        take_pooled(4 * COARSE)
        take(5 * COARSE, six_in, 0, COARSE)
        take(6 * COARSE, seven_a, 0, half)
        take(6 * COARSE + half, seven_b, 0, half)
        at = 7 * COARSE
        keys[pl.ds(at, COARSE)] = group_in[pl.ds(quad_at, COARSE), pl.ds(0, packed)]
        count = decode_count(group_in[pl.ds(quad_at, COARSE), pl.ds(packed, LANES)].astype(f32))
        bias[pl.ds(at, COARSE)] = jnp.where(count > 0, 0.0, MASKED)
        inverse[pl.ds(at, COARSE)] = 1.0 / jnp.maximum(count, 1.0)
        load_sums(group_in, half_group_at, 2 * COARSE, sums, counts, 0, coded=True)
        take_pooled(8 * COARSE)
        take(far_rows, sib, 0, BLOCK)
        take(far_rows + BLOCK, oth, 0, BLOCK)
        take(main_rows, sib_in, 0, BLOCK)
        take(main_rows + BLOCK, oth_in, 0, BLOCK)

        own_rows = (
            pl.ds(pl.multiple_of((1 - parity) * BLOCK, BLOCK), BLOCK),
            pl.ds(pl.multiple_of(parity * BLOCK, BLOCK), BLOCK),
        )
        nt = (((1,), (1,)), ((), ()))
        tn = (((0,), (0,)), ((), ()))
        segments = [(at, 64) for at in range(0, main_rows, 64)]
        halo_segments = [(at, 64) for at in range(0, BLOCK, 64)]

        def one_head(head):
            key_cols = pl.ds(pl.multiple_of(head * HEAD_DIM, HEAD_DIM), HEAD_DIM)
            value_cols = pl.ds(pl.multiple_of(width + head * HEAD_DIM, HEAD_DIM), HEAD_DIM)
            q = jnp.concatenate([query[r, key_cols] for r in own_rows], axis=0)
            c = jnp.concatenate([cot[r, key_cols] for r in own_rows], axis=0)

            def dots(cols, side):
                return (
                    lax.dot_general(keys[pl.ds(0, main_rows), cols], side, nt, preferred_element_type=f32),
                    lax.dot_general(
                        keys[pl.ds(main_rows, BLOCK), cols], side[:BLOCK], nt, preferred_element_type=f32
                    ),
                    lax.dot_general(
                        keys[pl.ds(main_rows + BLOCK, BLOCK), cols], side[BLOCK:], nt,
                        preferred_element_type=f32,
                    ),
                )

            main, near_sib, near_oth = dots(key_cols, q)
            score[pl.ds(0, main_rows)] = main * scale + by_lanes(bias[pl.ds(0, main_rows)], 2 * BLOCK)
            score[pl.ds(main_rows, BLOCK)] = jnp.concatenate(
                [
                    near_sib * scale + bias[pl.ds(main_rows, BLOCK)],
                    near_oth * scale + bias[pl.ds(main_rows + BLOCK, BLOCK)],
                ],
                axis=1,
            )
            main, near_sib, near_oth = dots(value_cols, c)
            grads[pl.ds(0, main_rows)] = main
            grads[pl.ds(main_rows, BLOCK)] = jnp.concatenate([near_sib, near_oth], axis=1)
            top = jnp.full((8, 2 * BLOCK), -jnp.inf, f32)
            for at in range(0, key_rows, 64):
                part = score[pl.ds(at, 64)]
                top = jnp.maximum(top, jnp.max(part.reshape(8, 8, 2 * BLOCK), axis=0))
            top = jnp.max(top, axis=0, keepdims=True)
            total = jnp.zeros((8, 2 * BLOCK), f32)
            mixed = jnp.zeros((8, 2 * BLOCK), f32)
            for at in range(0, key_rows, 64):
                e = jnp.exp(score[pl.ds(at, 64)] - top)
                score[pl.ds(at, 64)] = e
                total = total + jnp.sum(e.reshape(8, 8, 2 * BLOCK), axis=0)
                mixed = mixed + jnp.sum((e * grads[pl.ds(at, 64)]).reshape(8, 8, 2 * BLOCK), axis=0)
            total = 1.0 / jnp.sum(total, axis=0, keepdims=True)
            delta = jnp.sum(mixed, axis=0, keepdims=True) * total
            for at in range(0, key_rows, 64):
                prob = score[pl.ds(at, 64)] * total
                weight[pl.ds(at, 64), pl.ds(0, 2 * BLOCK)] = prob.astype(bf16)
                ds = prob * (grads[pl.ds(at, 64)] - delta)
                weight[pl.ds(at, 64), pl.ds(2 * BLOCK, 2 * BLOCK)] = ds.astype(bf16)

            def back(offset, cols):
                out = lax.dot_general(
                    weight[pl.ds(0, main_rows), pl.ds(offset, 2 * BLOCK)],
                    keys[pl.ds(0, main_rows), cols], tn, preferred_element_type=f32,
                )
                near = []
                for i in range(2):
                    near.append(
                        lax.dot_general(
                            weight[pl.ds(main_rows, BLOCK), pl.ds(offset + i * BLOCK, BLOCK)],
                            keys[pl.ds(main_rows + i * BLOCK, BLOCK), cols], tn,
                            preferred_element_type=f32,
                        )
                    )
                return out + jnp.concatenate(near, axis=0)

            out = back(0, value_cols)
            grad = back(2 * BLOCK, key_cols) * scale
            for i, r in enumerate(own_rows):
                attended[r, key_cols] = out[i * BLOCK : (i + 1) * BLOCK].astype(bf16)
                query_grad[r, key_cols] = grad[i * BLOCK : (i + 1) * BLOCK].astype(bf16)

            for offset, cols, side, factor in (
                (2 * BLOCK, key_cols, q, scale), (0, value_cols, c, None)
            ):
                res = jnp.dot(
                    weight[pl.ds(0, main_rows), pl.ds(offset, 2 * BLOCK)], side,
                    preferred_element_type=f32,
                )
                if factor is not None:
                    res = res * factor
                far = res[:far_rows] * inverse[...]
                own_grad[:, cols] = res[far_rows:]
                low_grad[:, cols] = far[: 2 * COARSE]
                three_out[:, cols] = far[2 * COARSE : 3 * COARSE].astype(bf16)
                shard_part[pl.ds(0, 2 * COARSE), cols] = far[3 * COARSE : 5 * COARSE]
                six_out[:, cols] = far[5 * COARSE : 6 * COARSE].astype(bf16)
                seven_a_out[:, cols] = far[6 * COARSE : 6 * COARSE + half].astype(bf16)
                seven_b_out[:, cols] = far[6 * COARSE + half : 7 * COARSE].astype(bf16)
                sums[head + (0 if offset else HEADS)] = far[7 * COARSE :]
                for i, out_ref in enumerate((sib_grad, oth_grad)):
                    near = jnp.dot(
                        weight[pl.ds(main_rows, BLOCK), pl.ds(offset + i * BLOCK, BLOCK)],
                        side[i * BLOCK : (i + 1) * BLOCK], preferred_element_type=f32,
                    )
                    if factor is not None:
                        near = near * factor
                    out_ref[:, cols] = near.astype(bf16)

        def step(head, carry):
            one_head(head)
            return carry

        lax.fori_loop(0, HEADS, step, 0)
        group_out[...] = jnp.zeros_like(group_out)
        for tile in range(sums.shape[0]):
            cols = pl.ds(tile * LANES, LANES)
            group_out[pl.ds(quad_at, COARSE), cols] = sums[tile, pl.ds(0, COARSE)].astype(bf16)
            wide = widen(sums[tile, pl.ds(COARSE, COARSE)], 2)
            group_out[pl.ds(half_group_at, 2 * COARSE), cols] = wide.astype(bf16)

    scratch = [
        pltpu.VMEM((key_rows + BLOCK, 2 * width), bf16),
        pltpu.VMEM((key_rows + BLOCK, LANES), f32),
        pltpu.VMEM((far_rows, LANES), f32),
        pltpu.VMEM((2 * width // LANES, 2 * COARSE, LANES), f32),
        pltpu.VMEM((2 * COARSE, LANES), f32),
        pltpu.VMEM((key_rows, 2 * BLOCK), f32),
        pltpu.VMEM((key_rows, 4 * BLOCK), bf16),
        pltpu.VMEM((key_rows, 2 * BLOCK), f32),
    ]
    outs = [
        shape(2 * BLOCK, width), shape(2 * BLOCK, width), shape(2 * BLOCK, 2 * width, f32),
        shape(BLOCK, 2 * width), shape(BLOCK, 2 * width), shape(2 * COARSE, 2 * width, f32),
        shape(COARSE, 2 * width), shape(2 * COARSE, 2 * width, f32), shape(COARSE, 2 * width),
        shape(half, 2 * width), shape(half, 2 * width), shape(group_rows, 2 * width),
    ]
    return kernel, outs, scratch


def widen(rows, times):
    count, width = rows.shape
    return jnp.broadcast_to(rows[:, None], (count, times, width)).reshape(count * times, width)


def back_kernel(
    index, part, six, seven_a, seven_b, group, three, low, sib_grad,
    out, sib_out, pair_a, pair_b, mine, acc,
):
    octet, half_shard = index[4], index[5]
    tile = six[...].astype(f32) + widen(seven_a[...].astype(f32) + seven_b[...].astype(f32), 2)
    few = COARSE // 4
    total = group[pl.ds(0, few)].astype(f32)
    for i in range(1, group.shape[0] // few):
        total = total + group[pl.ds(i * few, few)].astype(f32)
    tile = tile + widen(total, 4)
    acc[...] = widen(tile, out.shape[0] // COARSE)
    octet_at = pl.ds(pl.multiple_of(octet * COARSE, COARSE), COARSE)
    half_at = pl.ds(pl.multiple_of(half_shard * 2 * COARSE, 2 * COARSE), 2 * COARSE)
    acc[octet_at] = acc[octet_at] + part[pl.ds(0, COARSE)]
    acc[half_at] = acc[half_at] + widen(part[pl.ds(COARSE, COARSE)], 2)
    out[...] = acc[...].astype(bf16)
    half = COARSE // 2

    def quarter(bits):
        return three[pl.ds(quarter_at(index, bits), few)].astype(f32)

    sib_out[pl.ds(0, BLOCK)] = sib_grad[...]
    sib_out[pl.ds(BLOCK, COARSE)] = (low[pl.ds(0, COARSE)] + widen(quarter(1), 4)).astype(bf16)
    pair_a[...] = (low[pl.ds(COARSE, half)] + widen(quarter(2), 2)).astype(bf16)
    pair_b[...] = (low[pl.ds(COARSE + half, half)] + widen(quarter(3), 2)).astype(bf16)
    mine[...] = quarter(0)


def final_kernel(width):
    def kernel(
        index, mask, own, sib_back, oth_back, pair_a, pair_b, mine, shard,
        key_grad, value_grad, spread,
    ):
        parity = index[0]
        tokens = key_grad.shape[0]
        length = jnp.sum(mask[...], axis=1, keepdims=True)
        few = shard.shape[1]
        total = shard[0].astype(f32)
        for i in range(1, shard.shape[0]):
            total = total + shard[i].astype(f32)
        tile = widen(total, COARSE // few) + widen(mine[...], 4)
        tile = tile + widen(pair_a[...].astype(f32) + pair_b[...].astype(f32), 2)
        tile = tile + sib_back[pl.ds(BLOCK, COARSE)].astype(f32)
        spread[...] = widen(tile, tokens // COARSE)
        for i, (block, near) in enumerate(((1 - parity, sib_back), (parity, oth_back))):
            start = pl.multiple_of(block * BLOCK, BLOCK)
            live = (rows_of((BLOCK, LANES)) + start < length).astype(f32)
            grad = own[pl.ds(i * BLOCK, BLOCK)] + near[pl.ds(0, BLOCK)].astype(f32)
            grad = grad + spread[pl.ds(start, BLOCK)] * by_lanes(live, 2 * width)
            key_grad[pl.ds(start, BLOCK)] = grad[:, :width].astype(bf16)
            value_grad[pl.ds(start, BLOCK)] = grad[:, width:].astype(bf16)

    return kernel


def flip(count, bits):
    return [(i, i ^ bits) for i in range(count)]


def body(query_states, key_states, value_states, valid_mask, attended_grad):
    tokens, width = query_states.shape
    shards = lax.axis_size("shard")
    groups = lax.axis_size("grp")
    total = shards * groups
    packed = 2 * width
    row = packed + LANES
    half = COARSE // 2
    s = lax.axis_index("shard")
    g = lax.axis_index("grp")
    index = jnp.stack(
        [s & 1, s >> 1 & 1, s >> 2 & 1, s, s >> 3 ^ 1, s >> 4 ^ 1, g >> 2 ^ 1, g >> 3 ^ 1]
    ).astype(jnp.int32)
    mask = valid_mask.reshape(1, tokens)
    pairs = [(2 * i - 1, 2 * i) for i in range(1, total // 2)]
    pairs = pairs + [(high, low) for low, high in pairs]

    def on_shard(x, bits):
        return lax.ppermute(x, "shard", flip(shards, bits))

    def on_group(x, bits):
        return lax.ppermute(x, "grp", flip(groups, bits))

    few_shard = 2 * COARSE // 16
    few_group = COARSE // 4
    sib, oth, pair, gather = call(
        local_kernel(width, shards),
        [
            shape(BLOCK + COARSE, row), shape(BLOCK, row), shape(half, row),
            jax.ShapeDtypeStruct((shards, few_shard, row), bf16),
        ],
        [], index, mask, key_states, value_states, name="local",
    )
    sib_in = on_shard(sib, 1)
    pair_a = on_shard(pair, 2)
    pair_b = on_shard(pair, 3)
    oth_in = lax.ppermute(oth, ("grp", "shard"), pairs)
    shard_in = lax.all_to_all(gather, "shard", 0, 0, tiled=True).reshape(shards * few_shard, row)
    three, six, seven, wide = call(
        climb_kernel(groups),
        [
            shape(COARSE, row), shape(COARSE, row), shape(half, row),
            jax.ShapeDtypeStruct((groups, few_group, row), bf16),
        ],
        [
            pltpu.VMEM((packed // LANES, shards * few_shard, LANES), f32),
            pltpu.VMEM((shards * few_shard, LANES), f32),
        ],
        index, sib_in, pair, pair_a, pair_b, shard_in, name="climb",
    )
    six_in = on_group(six, 1)
    seven_a = on_group(seven, 2)
    seven_b = on_group(seven, 3)
    three_in = on_shard(three, 4)
    group_in = lax.all_to_all(wide, "grp", 0, 0, tiled=True).reshape(groups * few_group, row)
    kernel, outs, scratch = attention_kernel(width, shards * few_shard, groups * few_group)
    (
        attended, query_grad, own_grad, sib_grad, oth_grad, low_grad, three_out, shard_part,
        six_out, seven_a_out, seven_b_out, group_out,
    ) = call(
        kernel, outs, scratch, index, query_states, attended_grad, sib, oth, sib_in, oth_in,
        pair_a, pair_b, three_in, shard_in, six_in, seven_a, seven_b, group_in,
        flops=1_600_000_000, name="attention",
    )
    six_back = on_group(six_out, 1)
    seven_a_back = on_group(seven_a_out, 2)
    seven_b_back = on_group(seven_b_out, 3)
    three_back = on_shard(three_out, 4)
    oth_back = lax.ppermute(oth_grad, ("grp", "shard"), pairs)
    group_back = lax.all_to_all(group_out, "grp", 0, 0, tiled=True)
    shard_out, sib_out, pair_a_out, pair_b_out, mine = call(
        back_kernel,
        [
            shape(shards * few_shard, packed), shape(BLOCK + COARSE, packed),
            shape(half, packed), shape(half, packed), shape(few_group, packed, f32),
        ],
        [pltpu.VMEM((shards * few_shard, packed), f32)],
        index, shard_part, six_back, seven_a_back, seven_b_back, group_back, three_back,
        low_grad, sib_grad, name="back",
    )
    sib_back = on_shard(sib_out, 1)
    pair_a_back = on_shard(pair_a_out, 2)
    pair_b_back = on_shard(pair_b_out, 3)
    shard_back = lax.all_to_all(shard_out, "shard", 0, 0, tiled=True)
    key_grad, value_grad = call(
        final_kernel(width), [shape(tokens, width), shape(tokens, width)],
        [pltpu.VMEM((tokens, packed), f32)],
        index, mask, own_grad, sib_back, oth_back, pair_a_back, pair_b_back, mine,
        shard_back.reshape(shards, few_shard, packed), name="final",
    )
    return attended, query_grad, key_grad, value_grad


def solution(mesh):
    whole = P(("grp", "shard"), None)
    return jax.shard_map(
        body,
        mesh=mesh,
        in_specs=(whole, whole, whole, P(("grp", "shard")), whole),
        out_specs=(whole, whole, whole, whole),
        check_vma=False,
    )
```

```python
import jax
import jax.numpy as jnp
from jax import lax
from jax.experimental import pallas as pl
from jax.experimental.pallas import tpu as pltpu
from jax.sharding import PartitionSpec as P

HEADS = 4
HEAD_DIM = 128
BLOCK = 128
COARSE = 64
LEVELS = 9
LANES = 128
MASKED = -1e30
VMEM_BYTES = 56 * 1024 * 1024

f32 = jnp.float32
bf16 = jnp.bfloat16


def rows_of(shape):
    return lax.broadcasted_iota(jnp.int32, shape, 0)


def call(kernel, outs, scratch, index, *operands, flops=0, name=None):
    size = sum(o.size * o.dtype.itemsize for o in operands)
    size += sum(o.size * o.dtype.itemsize for o in outs)
    in_specs = [pl.BlockSpec(memory_space=pltpu.SMEM)]
    in_specs += [pl.BlockSpec(memory_space=pltpu.VMEM) for _ in operands]
    return pl.pallas_call(
        kernel,
        out_shape=outs,
        in_specs=in_specs,
        out_specs=[pl.BlockSpec(memory_space=pltpu.VMEM) for _ in outs],
        scratch_shapes=scratch,
        compiler_params=pltpu.CompilerParams(vmem_limit_bytes=VMEM_BYTES),
        cost_estimate=pl.CostEstimate(flops=flops, bytes_accessed=size, transcendentals=0),
        name=name,
    )(index, *operands)


def shape(rows, width, dtype=bf16):
    return jax.ShapeDtypeStruct((rows, width), dtype)


def by_lanes(column, width):
    return jnp.concatenate([column] * (width // LANES), axis=1)


def local_kernel(width, peers):
    def kernel(index, mask, key, value, sib, oth, pair, gather):
        parity = index[0]
        tokens = key.shape[0]
        length = jnp.sum(mask[...], axis=1, keepdims=True)
        for ref, block in ((sib, 1 - parity), (oth, parity)):
            start = pl.multiple_of(block * BLOCK, BLOCK)
            ref[pl.ds(0, BLOCK), pl.ds(0, width)] = key[pl.ds(start, BLOCK)]
            ref[pl.ds(0, BLOCK), pl.ds(width, width)] = value[pl.ds(start, BLOCK)]
            place = rows_of((BLOCK, LANES)) + start
            ref[pl.ds(0, BLOCK), pl.ds(2 * width, LANES)] = (place < length).astype(f32).astype(bf16)

        def means(rows):
            group = tokens // rows
            row = rows_of((rows, tokens))
            place = lax.broadcasted_iota(jnp.int32, (rows, tokens), 1)
            member = (row * group <= place) & (place < row * group + group) & (place < length)
            member = member.astype(f32).astype(bf16)
            first = rows_of((rows, LANES)) * group
            count = jnp.clip(length - first, 0, group).astype(f32)
            inverse = by_lanes(1.0 / jnp.maximum(count, 1.0), width)
            k_sum = jnp.dot(member, key[...], preferred_element_type=f32)
            v_sum = jnp.dot(member, value[...], preferred_element_type=f32)
            return (k_sum * inverse).astype(bf16), (v_sum * inverse).astype(bf16), count.astype(bf16)

        k_mean, v_mean, count = means(COARSE)
        sib[pl.ds(BLOCK, COARSE), pl.ds(0, width)] = k_mean
        sib[pl.ds(BLOCK, COARSE), pl.ds(width, width)] = v_mean
        sib[pl.ds(BLOCK, COARSE), pl.ds(2 * width, LANES)] = count
        k_mean, v_mean, count = means(COARSE // 2)
        pair[:, pl.ds(0, width)] = k_mean
        pair[:, pl.ds(width, width)] = v_mean
        pair[:, pl.ds(2 * width, LANES)] = count
        few = gather.shape[1]
        k_mean, v_mean, count = means(few)
        for peer in range(peers):
            gather[peer, :, pl.ds(0, width)] = k_mean
            gather[peer, :, pl.ds(width, width)] = v_mean
            gather[peer, :, pl.ds(2 * width, LANES)] = count

    return kernel


def store_means(out, first, sums, count, scale_width):
    inverse = by_lanes(1.0 / jnp.maximum(count, 1.0), scale_width)
    rows = count.shape[0]
    out[pl.ds(first, rows), pl.ds(0, scale_width)] = (sums * inverse).astype(bf16)
    out[pl.ds(first, rows), pl.ds(scale_width, LANES)] = count.astype(bf16)


def load_sums(ref, first, rows, sums, counts, at):
    width = sums.shape[0] * LANES
    count = ref[pl.ds(first, rows), pl.ds(width, LANES)].astype(f32)
    counts[pl.ds(at, rows)] = count
    for tile in range(sums.shape[0]):
        mean = ref[pl.ds(first, rows), pl.ds(tile * LANES, LANES)].astype(f32)
        sums[tile, pl.ds(at, rows)] = mean * count


def pooled(ref, rows, step, base=0):
    if len(ref.shape) == 3:
        return jnp.concatenate(
            [pooled(ref.at[tile], rows, step, base) for tile in range(ref.shape[0])], axis=1
        )
    total = ref[pl.ds(base, rows, stride=step)]
    for i in range(1, step):
        total = total + ref[pl.ds(base + i, rows, stride=step)]
    return total


def quarter_at(index, flip_bits):
    few = COARSE // 4
    return pl.multiple_of(((index[3] & 3) ^ flip_bits) * few, few)


def climb_kernel(groups):
    def kernel(
        index, sib_in, pair, pair_a, pair_b, recv, three, six, seven, wide, shares, sums, counts
    ):
        width = sums.shape[0] * LANES
        total = recv.shape[0]
        load_sums(recv, 0, total, sums, counts, 0)
        quarter = total // COARSE
        store_means(six, 0, pooled(sums, COARSE, quarter), pooled(counts, COARSE, quarter), width)
        half = COARSE // 2
        store_means(
            seven, 0, pooled(sums, half, 2 * quarter), pooled(counts, half, 2 * quarter), width
        )
        far_half = index[7]
        held = wide.shape[1]
        for side, rows in ((1 - far_half, held), (far_half, held // 2)):
            count = pooled(counts, rows, total // rows)
            share = 1.0 / jnp.maximum(count, 1.0)
            mean = pooled(sums, rows, total // rows) * by_lanes(share, width)
            if rows < held:
                shares[pl.ds(held, rows)] = share
                mean = jnp.concatenate([mean, jnp.zeros_like(mean)], axis=0)
            else:
                shares[pl.ds(0, rows)] = share
            for i in range(groups // 2):
                wide[side * (groups // 2) + i] = mean.astype(bf16)
        few = COARSE // 4
        for ref, first, rows, bits in (
            (pair, 0, half, 0), (sib_in, BLOCK, COARSE, 1), (pair_a, 0, half, 2), (pair_b, 0, half, 3)
        ):
            base = bits * COARSE
            load_sums(ref, first, rows, sums, counts, base)
            step = rows // few
            store_means(
                three, quarter_at(index, bits), pooled(sums, few, step, base),
                pooled(counts, few, step, base), width,
            )

    return kernel


def attention_kernel(width, shard_rows, group_rows):
    far_rows = LEVELS * COARSE
    scale = HEAD_DIM**-0.5
    main_rows = far_rows + 2 * BLOCK
    key_rows = main_rows + BLOCK
    half = COARSE // 2

    def kernel(
        index, query, cot, sib, oth, sib_in, oth_in, pair_a, pair_b, three_in, shard_in, six_in,
        seven_a, seven_b, group_in,
        attended, query_grad, own_grad, sib_grad, oth_grad, low_grad, three_out,
        shard_part, six_out, seven_a_out, seven_b_out, group_out,
        keys, bias, inverse, sums, counts, score, weight, grads,
    ):
        parity, octet, half_shard, quad_group, half_group = (
            index[0], index[4], index[5], index[6], index[7]
        )
        packed = 2 * width

        def take(at, ref, first, rows):
            keys[pl.ds(at, rows)] = ref[pl.ds(first, rows), pl.ds(0, packed)]
            count = ref[pl.ds(first, rows), pl.ds(packed, LANES)].astype(f32)
            bias[pl.ds(at, rows)] = jnp.where(count > 0, 0.0, MASKED)
            if at < far_rows:
                inverse[pl.ds(at, rows)] = 1.0 / jnp.maximum(count, 1.0)

        def take_pooled(at):
            count = pooled(counts, COARSE, 2)
            inv = 1.0 / jnp.maximum(count, 1.0)
            keys[pl.ds(at, COARSE)] = (pooled(sums, COARSE, 2) * by_lanes(inv, packed)).astype(bf16)
            bias[pl.ds(at, COARSE)] = jnp.where(count > 0, 0.0, MASKED)
            inverse[pl.ds(at, COARSE)] = inv

        octet_at = pl.multiple_of(octet * COARSE, COARSE)
        half_shard_at = pl.multiple_of(half_shard * 2 * COARSE, 2 * COARSE)
        quad_at = pl.multiple_of(quad_group * COARSE, COARSE)
        half_group_at = pl.multiple_of(half_group * 2 * COARSE, 2 * COARSE)
        take(0, sib_in, BLOCK, COARSE)
        take(COARSE, pair_a, 0, half)
        take(COARSE + half, pair_b, 0, half)
        take(2 * COARSE, three_in, 0, COARSE)
        take(3 * COARSE, shard_in, octet_at, COARSE)
        load_sums(shard_in, half_shard_at, 2 * COARSE, sums, counts, 0)
        take_pooled(4 * COARSE)
        take(5 * COARSE, six_in, 0, COARSE)
        take(6 * COARSE, seven_a, 0, half)
        take(6 * COARSE + half, seven_b, 0, half)
        at = 7 * COARSE
        keys[pl.ds(at, COARSE)] = group_in[pl.ds(quad_at, COARSE)]
        nine = group_in[pl.ds(half_group_at, 2 * COARSE)].astype(f32)
        nine = nine.reshape(8, 2 * COARSE // 8, packed)[:, : COARSE // 8].reshape(COARSE, packed)
        keys[pl.ds(at + COARSE, COARSE)] = nine.astype(bf16)
        bias[pl.ds(at, 2 * COARSE)] = jnp.zeros((2 * COARSE, LANES), f32)
        inverse[pl.ds(at, 2 * COARSE)] = jnp.ones((2 * COARSE, LANES), f32)
        take(far_rows, sib, 0, BLOCK)
        take(far_rows + BLOCK, oth, 0, BLOCK)
        take(main_rows, sib_in, 0, BLOCK)
        take(main_rows + BLOCK, oth_in, 0, BLOCK)

        own_rows = (
            pl.ds(pl.multiple_of((1 - parity) * BLOCK, BLOCK), BLOCK),
            pl.ds(pl.multiple_of(parity * BLOCK, BLOCK), BLOCK),
        )
        nt = (((1,), (1,)), ((), ()))
        tn = (((0,), (0,)), ((), ()))
        segments = [(at, 64) for at in range(0, main_rows, 64)]
        halo_segments = [(at, 64) for at in range(0, BLOCK, 64)]

        def one_head(head):
            key_cols = pl.ds(head * HEAD_DIM, HEAD_DIM)
            value_cols = pl.ds(width + head * HEAD_DIM, HEAD_DIM)
            q = jnp.concatenate([query[r, key_cols] for r in own_rows], axis=0)
            c = jnp.concatenate([cot[r, key_cols] for r in own_rows], axis=0)

            def dots(cols, side):
                return (
                    lax.dot_general(keys[pl.ds(0, main_rows), cols], side, nt, preferred_element_type=f32),
                    lax.dot_general(
                        keys[pl.ds(main_rows, BLOCK), cols], side[:BLOCK], nt, preferred_element_type=f32
                    ),
                    lax.dot_general(
                        keys[pl.ds(main_rows + BLOCK, BLOCK), cols], side[BLOCK:], nt,
                        preferred_element_type=f32,
                    ),
                )

            main, near_sib, near_oth = dots(key_cols, q)
            score[pl.ds(0, main_rows)] = main * scale + by_lanes(bias[pl.ds(0, main_rows)], 2 * BLOCK)
            score[pl.ds(main_rows, BLOCK)] = jnp.concatenate(
                [
                    near_sib * scale + bias[pl.ds(main_rows, BLOCK)],
                    near_oth * scale + bias[pl.ds(main_rows + BLOCK, BLOCK)],
                ],
                axis=1,
            )
            main, near_sib, near_oth = dots(value_cols, c)
            grads[pl.ds(0, main_rows)] = main
            grads[pl.ds(main_rows, BLOCK)] = jnp.concatenate([near_sib, near_oth], axis=1)
            top = jnp.full((8, 2 * BLOCK), -jnp.inf, f32)
            for at in range(0, key_rows, 64):
                part = score[pl.ds(at, 64)]
                top = jnp.maximum(top, jnp.max(part.reshape(8, 8, 2 * BLOCK), axis=0))
            top = jnp.max(top, axis=0, keepdims=True)
            total = jnp.zeros((8, 2 * BLOCK), f32)
            mixed = jnp.zeros((8, 2 * BLOCK), f32)
            for at in range(0, key_rows, 64):
                e = jnp.exp(score[pl.ds(at, 64)] - top)
                score[pl.ds(at, 64)] = e
                total = total + jnp.sum(e.reshape(8, 8, 2 * BLOCK), axis=0)
                mixed = mixed + jnp.sum((e * grads[pl.ds(at, 64)]).reshape(8, 8, 2 * BLOCK), axis=0)
            total = 1.0 / jnp.sum(total, axis=0, keepdims=True)
            delta = jnp.sum(mixed, axis=0, keepdims=True) * total
            for at in range(0, key_rows, 64):
                prob = score[pl.ds(at, 64)] * total
                weight[pl.ds(at, 64), pl.ds(0, 2 * BLOCK)] = prob.astype(bf16)
                ds = prob * (grads[pl.ds(at, 64)] - delta)
                weight[pl.ds(at, 64), pl.ds(2 * BLOCK, 2 * BLOCK)] = ds.astype(bf16)

            def back(offset, cols):
                out = lax.dot_general(
                    weight[pl.ds(0, main_rows), pl.ds(offset, 2 * BLOCK)],
                    keys[pl.ds(0, main_rows), cols], tn, preferred_element_type=f32,
                )
                near = []
                for i in range(2):
                    near.append(
                        lax.dot_general(
                            weight[pl.ds(main_rows, BLOCK), pl.ds(offset + i * BLOCK, BLOCK)],
                            keys[pl.ds(main_rows + i * BLOCK, BLOCK), cols], tn,
                            preferred_element_type=f32,
                        )
                    )
                return out + jnp.concatenate(near, axis=0)

            out = back(0, value_cols)
            grad = back(2 * BLOCK, key_cols) * scale
            for i, r in enumerate(own_rows):
                attended[r, key_cols] = out[i * BLOCK : (i + 1) * BLOCK].astype(bf16)
                query_grad[r, key_cols] = grad[i * BLOCK : (i + 1) * BLOCK].astype(bf16)

            for offset, cols, side, factor in (
                (2 * BLOCK, key_cols, q, scale), (0, value_cols, c, None)
            ):
                res = jnp.dot(
                    weight[pl.ds(0, main_rows), pl.ds(offset, 2 * BLOCK)], side,
                    preferred_element_type=f32,
                )
                if factor is not None:
                    res = res * factor
                far = res[:far_rows] * inverse[...]
                own_grad[:, cols] = res[far_rows:]
                low_grad[:, cols] = far[: 2 * COARSE]
                three_out[:, cols] = far[2 * COARSE : 3 * COARSE].astype(bf16)
                shard_part[pl.ds(0, 2 * COARSE), cols] = far[3 * COARSE : 5 * COARSE]
                six_out[:, cols] = far[5 * COARSE : 6 * COARSE].astype(bf16)
                seven_a_out[:, cols] = far[6 * COARSE : 6 * COARSE + half].astype(bf16)
                seven_b_out[:, cols] = far[6 * COARSE + half : 7 * COARSE].astype(bf16)
                sums[head + (0 if offset else HEADS)] = far[7 * COARSE :]
                for i, out_ref in enumerate((sib_grad, oth_grad)):
                    near = jnp.dot(
                        weight[pl.ds(main_rows, BLOCK), pl.ds(offset + i * BLOCK, BLOCK)],
                        side[i * BLOCK : (i + 1) * BLOCK], preferred_element_type=f32,
                    )
                    if factor is not None:
                        near = near * factor
                    out_ref[:, cols] = near.astype(bf16)

        for head in range(HEADS):
            one_head(head)
        group_out[...] = jnp.zeros_like(group_out)
        for tile in range(sums.shape[0]):
            cols = pl.ds(tile * LANES, LANES)
            group_out[pl.ds(quad_at, COARSE), cols] = sums[tile, pl.ds(0, COARSE)].astype(bf16)
            nine = sums[tile, pl.ds(COARSE, COARSE)].reshape(8, COARSE // 8, LANES)
            wide = jnp.concatenate([nine, jnp.zeros_like(nine)], axis=1).reshape(2 * COARSE, LANES)
            group_out[pl.ds(half_group_at, 2 * COARSE), cols] = wide.astype(bf16)

    scratch = [
        pltpu.VMEM((key_rows + BLOCK, 2 * width), bf16),
        pltpu.VMEM((key_rows + BLOCK, LANES), f32),
        pltpu.VMEM((far_rows, LANES), f32),
        pltpu.VMEM((2 * width // LANES, 2 * COARSE, LANES), f32),
        pltpu.VMEM((2 * COARSE, LANES), f32),
        pltpu.VMEM((key_rows, 2 * BLOCK), f32),
        pltpu.VMEM((key_rows, 4 * BLOCK), bf16),
        pltpu.VMEM((key_rows, 2 * BLOCK), f32),
    ]
    outs = [
        shape(2 * BLOCK, width), shape(2 * BLOCK, width), shape(2 * BLOCK, 2 * width, f32),
        shape(BLOCK, 2 * width), shape(BLOCK, 2 * width), shape(2 * COARSE, 2 * width, f32),
        shape(COARSE, 2 * width), shape(2 * COARSE, 2 * width, f32), shape(COARSE, 2 * width),
        shape(half, 2 * width), shape(half, 2 * width), shape(group_rows, 2 * width),
    ]
    return kernel, outs, scratch


def widen(rows, times):
    count, width = rows.shape
    return jnp.broadcast_to(rows[:, None], (count, times, width)).reshape(count * times, width)


def back_kernel(
    index, part, six, seven_a, seven_b, group, shares, three, low, sib_grad,
    out, sib_out, pair_a, pair_b, mine, acc,
):
    octet, half_shard = index[4], index[5]
    tile = six[...].astype(f32) + widen(seven_a[...].astype(f32) + seven_b[...].astype(f32), 2)
    few = COARSE // 4
    quad_at = pl.multiple_of(index[6] * COARSE, COARSE)
    half_at = pl.multiple_of(index[7] * 2 * COARSE, 2 * COARSE)
    eight = jnp.sum(group[pl.ds(quad_at, COARSE)].astype(f32).reshape(4, few, -1), axis=0)
    nine = group[pl.ds(half_at, 2 * COARSE)].astype(f32).reshape(8, few, -1)[:, : few // 2]
    nine = jnp.sum(nine, axis=0)
    share = by_lanes(shares[...], tile.shape[1])
    tile = tile + widen(eight * share[:few], 4) + widen(nine * share[few : few + few // 2], 8)
    acc[...] = widen(tile, out.shape[0] // COARSE)
    octet_at = pl.ds(pl.multiple_of(octet * COARSE, COARSE), COARSE)
    half_at = pl.ds(pl.multiple_of(half_shard * 2 * COARSE, 2 * COARSE), 2 * COARSE)
    acc[octet_at] = acc[octet_at] + part[pl.ds(0, COARSE)]
    acc[half_at] = acc[half_at] + widen(part[pl.ds(COARSE, COARSE)], 2)
    out[...] = acc[...].astype(bf16)
    half = COARSE // 2

    def quarter(bits):
        return three[pl.ds(quarter_at(index, bits), few)].astype(f32)

    sib_out[pl.ds(0, BLOCK)] = sib_grad[...]
    sib_out[pl.ds(BLOCK, COARSE)] = (low[pl.ds(0, COARSE)] + widen(quarter(1), 4)).astype(bf16)
    pair_a[...] = (low[pl.ds(COARSE, half)] + widen(quarter(2), 2)).astype(bf16)
    pair_b[...] = (low[pl.ds(COARSE + half, half)] + widen(quarter(3), 2)).astype(bf16)
    mine[...] = quarter(0)


def final_kernel(width):
    def kernel(
        index, mask, own, sib_back, oth_back, pair_a, pair_b, mine, shard,
        key_grad, value_grad, spread,
    ):
        parity = index[0]
        tokens = key_grad.shape[0]
        length = jnp.sum(mask[...], axis=1, keepdims=True)
        few = shard.shape[1]
        total = shard[0].astype(f32)
        for i in range(1, shard.shape[0]):
            total = total + shard[i].astype(f32)
        tile = widen(total, COARSE // few) + widen(mine[...], 4)
        tile = tile + widen(pair_a[...].astype(f32) + pair_b[...].astype(f32), 2)
        tile = tile + sib_back[pl.ds(BLOCK, COARSE)].astype(f32)
        spread[...] = widen(tile, tokens // COARSE)
        for i, (block, near) in enumerate(((1 - parity, sib_back), (parity, oth_back))):
            start = pl.multiple_of(block * BLOCK, BLOCK)
            live = (rows_of((BLOCK, LANES)) + start < length).astype(f32)
            grad = own[pl.ds(i * BLOCK, BLOCK)] + near[pl.ds(0, BLOCK)].astype(f32)
            grad = grad + spread[pl.ds(start, BLOCK)] * by_lanes(live, 2 * width)
            key_grad[pl.ds(start, BLOCK)] = grad[:, :width].astype(bf16)
            value_grad[pl.ds(start, BLOCK)] = grad[:, width:].astype(bf16)

    return kernel


def flip(count, bits):
    return [(i, i ^ bits) for i in range(count)]


def body(query_states, key_states, value_states, valid_mask, attended_grad):
    tokens, width = query_states.shape
    shards = lax.axis_size("shard")
    groups = lax.axis_size("grp")
    total = shards * groups
    packed = 2 * width
    row = packed + LANES
    half = COARSE // 2
    s = lax.axis_index("shard")
    g = lax.axis_index("grp")
    index = jnp.stack(
        [s & 1, s >> 1 & 1, s >> 2 & 1, s, s >> 3 ^ 1, s >> 4 ^ 1, g >> 2 ^ 1, g >> 3 ^ 1]
    ).astype(jnp.int32)
    mask = valid_mask.reshape(1, tokens)
    pairs = [(2 * i - 1, 2 * i) for i in range(1, total // 2)]
    pairs = pairs + [(high, low) for low, high in pairs]

    def on_shard(x, bits):
        return lax.ppermute(x, "shard", flip(shards, bits))

    def on_group(x, bits):
        return lax.ppermute(x, "grp", flip(groups, bits))

    few_shard = 2 * COARSE // 16
    few_group = COARSE // 4
    sib, oth, pair, gather = call(
        local_kernel(width, shards),
        [
            shape(BLOCK + COARSE, row), shape(BLOCK, row), shape(half, row),
            jax.ShapeDtypeStruct((shards, few_shard, row), bf16),
        ],
        [], index, mask, key_states, value_states, name="local",
    )
    sib_in = on_shard(sib, 1)
    pair_a = on_shard(pair, 2)
    pair_b = on_shard(pair, 3)
    oth_in = lax.ppermute(oth, ("grp", "shard"), pairs)
    shard_in = lax.all_to_all(gather, "shard", 0, 0, tiled=True).reshape(shards * few_shard, row)
    three, six, seven, wide, shares = call(
        climb_kernel(groups),
        [
            shape(COARSE, row), shape(COARSE, row), shape(half, row),
            jax.ShapeDtypeStruct((groups, few_group, packed), bf16),
            shape(few_group + few_group // 2, LANES, f32),
        ],
        [
            pltpu.VMEM((packed // LANES, shards * few_shard, LANES), f32),
            pltpu.VMEM((shards * few_shard, LANES), f32),
        ],
        index, sib_in, pair, pair_a, pair_b, shard_in, name="climb",
    )
    six_in = on_group(six, 1)
    seven_a = on_group(seven, 2)
    seven_b = on_group(seven, 3)
    three_in = on_shard(three, 4)
    group_in = lax.all_to_all(wide, "grp", 0, 0, tiled=True).reshape(groups * few_group, packed)
    kernel, outs, scratch = attention_kernel(width, shards * few_shard, groups * few_group)
    (
        attended, query_grad, own_grad, sib_grad, oth_grad, low_grad, three_out, shard_part,
        six_out, seven_a_out, seven_b_out, group_out,
    ) = call(
        kernel, outs, scratch, index, query_states, attended_grad, sib, oth, sib_in, oth_in,
        pair_a, pair_b, three_in, shard_in, six_in, seven_a, seven_b, group_in,
        flops=1_600_000_000, name="attention",
    )
    six_back = on_group(six_out, 1)
    seven_a_back = on_group(seven_a_out, 2)
    seven_b_back = on_group(seven_b_out, 3)
    three_back = on_shard(three_out, 4)
    oth_back = lax.ppermute(oth_grad, ("grp", "shard"), pairs)
    group_back = lax.all_to_all(group_out, "grp", 0, 0, tiled=True)
    oth_back, group_back = lax.optimization_barrier((oth_back, group_back))
    shard_out, sib_out, pair_a_out, pair_b_out, mine = call(
        back_kernel,
        [
            shape(shards * few_shard, packed), shape(BLOCK + COARSE, packed),
            shape(half, packed), shape(half, packed), shape(few_group, packed, f32),
        ],
        [pltpu.VMEM((shards * few_shard, packed), f32)],
        index, shard_part, six_back, seven_a_back, seven_b_back, group_back, shares, three_back,
        low_grad, sib_grad, name="back",
    )
    sib_back = on_shard(sib_out, 1)
    pair_a_back = on_shard(pair_a_out, 2)
    pair_b_back = on_shard(pair_b_out, 3)
    shard_back = lax.all_to_all(shard_out, "shard", 0, 0, tiled=True)
    key_grad, value_grad = call(
        final_kernel(width), [shape(tokens, width), shape(tokens, width)],
        [pltpu.VMEM((tokens, packed), f32)],
        index, mask, own_grad, sib_back, oth_back, pair_a_back, pair_b_back, mine,
        shard_back.reshape(shards, few_shard, packed), name="final",
    )
    return attended, query_grad, key_grad, value_grad


def solution(mesh):
    whole = P(("grp", "shard"), None)
    return jax.shard_map(
        body,
        mesh=mesh,
        in_specs=(whole, whole, whole, P(("grp", "shard")), whole),
        out_specs=(whole, whole, whole, whole),
        check_vma=False,
    )
```

```python
import jax
import jax.numpy as jnp
from jax import lax
from jax.experimental import pallas as pl
from jax.experimental.pallas import tpu as pltpu
from jax.sharding import PartitionSpec as P

HEADS = 4
HEAD_DIM = 128
BLOCK = 128
COARSE = 64
LEVELS = 9
LANES = 128
MASKED = -1e30
VMEM_BYTES = 56 * 1024 * 1024

f32 = jnp.float32
bf16 = jnp.bfloat16


def coordinate(index, item):
    device = index[0]
    shard = device & 31
    group = device >> 5
    if item == 3:
        return shard
    if item < 3:
        return shard >> item & 1
    if item < 6:
        return shard >> (item - 1) ^ 1
    return group >> (item - 4) ^ 1


def rows_of(shape):
    return lax.broadcasted_iota(jnp.int32, shape, 0)


def call(kernel, outs, scratch, index, *operands, flops=0, name=None, room=8):
    size = sum(o.size * o.dtype.itemsize for o in operands)
    size += sum(o.size * o.dtype.itemsize for o in outs)
    in_specs = [pl.BlockSpec(memory_space=pltpu.SMEM)]
    in_specs += [pl.BlockSpec(memory_space=pltpu.VMEM) for _ in operands]
    return pl.pallas_call(
        kernel,
        out_shape=outs,
        in_specs=in_specs,
        out_specs=[pl.BlockSpec(memory_space=pltpu.VMEM) for _ in outs],
        scratch_shapes=scratch,
        compiler_params=pltpu.CompilerParams(vmem_limit_bytes=room * 1024 * 1024),
        cost_estimate=pl.CostEstimate(flops=flops, bytes_accessed=size, transcendentals=0),
        name=name,
    )(index, *operands)


def shape(rows, width, dtype=bf16):
    return jax.ShapeDtypeStruct((rows, width), dtype)


def by_lanes(column, width):
    return jnp.concatenate([column] * (width // LANES), axis=1)


def local_kernel(width, peers):
    def kernel(index, mask, key, value, sib, oth, pair, gather):
        parity = coordinate(index, 0)
        tokens = key.shape[0]
        length = jnp.sum(mask[...], axis=1, keepdims=True)
        for ref, block in ((sib, 1 - parity), (oth, parity)):
            start = pl.multiple_of(block * BLOCK, BLOCK)
            ref[pl.ds(0, BLOCK), pl.ds(0, width)] = key[pl.ds(start, BLOCK)]
            ref[pl.ds(0, BLOCK), pl.ds(width, width)] = value[pl.ds(start, BLOCK)]
            place = rows_of((BLOCK, LANES)) + start
            ref[pl.ds(0, BLOCK), pl.ds(2 * width, LANES)] = (place < length).astype(f32).astype(bf16)

        def means(rows):
            group = tokens // rows
            row = rows_of((rows, tokens))
            place = lax.broadcasted_iota(jnp.int32, (rows, tokens), 1)
            member = (row * group <= place) & (place < row * group + group) & (place < length)
            member = member.astype(f32).astype(bf16)
            first = rows_of((rows, LANES)) * group
            count = jnp.clip(length - first, 0, group).astype(f32)
            inverse = by_lanes(1.0 / jnp.maximum(count, 1.0), width)
            k_sum = jnp.dot(member, key[...], preferred_element_type=f32)
            v_sum = jnp.dot(member, value[...], preferred_element_type=f32)
            return (k_sum * inverse).astype(bf16), (v_sum * inverse).astype(bf16), count.astype(bf16)

        k_mean, v_mean, count = means(COARSE)
        sib[pl.ds(BLOCK, COARSE), pl.ds(0, width)] = k_mean
        sib[pl.ds(BLOCK, COARSE), pl.ds(width, width)] = v_mean
        sib[pl.ds(BLOCK, COARSE), pl.ds(2 * width, LANES)] = count
        k_mean, v_mean, count = means(COARSE // 2)
        pair[:, pl.ds(0, width)] = k_mean
        pair[:, pl.ds(width, width)] = v_mean
        pair[:, pl.ds(2 * width, LANES)] = count
        few = gather.shape[1]
        k_mean, v_mean, count = means(few)
        for peer in range(peers):
            gather[peer, :, pl.ds(0, width)] = k_mean
            gather[peer, :, pl.ds(width, width)] = v_mean
            gather[peer, :, pl.ds(2 * width, LANES)] = count

    return kernel


def store_means(out, first, sums, count, scale_width):
    inverse = by_lanes(1.0 / jnp.maximum(count, 1.0), scale_width)
    rows = count.shape[0]
    out[pl.ds(first, rows), pl.ds(0, scale_width)] = (sums * inverse).astype(bf16)
    out[pl.ds(first, rows), pl.ds(scale_width, LANES)] = count.astype(bf16)


def load_sums(ref, first, rows, sums, counts, at):
    width = sums.shape[0] * LANES
    count = ref[pl.ds(first, rows), pl.ds(width, LANES)].astype(f32)
    counts[pl.ds(at, rows)] = count
    for tile in range(sums.shape[0]):
        mean = ref[pl.ds(first, rows), pl.ds(tile * LANES, LANES)].astype(f32)
        sums[tile, pl.ds(at, rows)] = mean * count


def pooled(ref, rows, step, base=0):
    if len(ref.shape) == 3:
        return jnp.concatenate(
            [pooled(ref.at[tile], rows, step, base) for tile in range(ref.shape[0])], axis=1
        )
    total = ref[pl.ds(base, rows, stride=step)]
    for i in range(1, step):
        total = total + ref[pl.ds(base + i, rows, stride=step)]
    return total


def quarter_at(index, flip_bits):
    few = COARSE // 4
    return pl.multiple_of(((coordinate(index, 3) & 3) ^ flip_bits) * few, few)


def climb_kernel(groups):
    def kernel(
        index, sib_in, pair, pair_a, pair_b, recv, three, six, seven, wide, shares, sums, counts
    ):
        width = sums.shape[0] * LANES
        total = recv.shape[0]
        load_sums(recv, 0, total, sums, counts, 0)
        quarter = total // COARSE
        store_means(six, 0, pooled(sums, COARSE, quarter), pooled(counts, COARSE, quarter), width)
        half = COARSE // 2
        store_means(
            seven, 0, pooled(sums, half, 2 * quarter), pooled(counts, half, 2 * quarter), width
        )
        far_half = coordinate(index, 7)
        held = wide.shape[1]
        for side, rows in ((1 - far_half, held), (far_half, held // 2)):
            count = pooled(counts, rows, total // rows)
            share = 1.0 / jnp.maximum(count, 1.0)
            mean = pooled(sums, rows, total // rows) * by_lanes(share, width)
            if rows < held:
                shares[pl.ds(held, rows)] = share
                mean = jnp.concatenate([mean, jnp.zeros_like(mean)], axis=0)
            else:
                shares[pl.ds(0, rows)] = share
            for i in range(groups // 2):
                wide[side * (groups // 2) + i] = mean.astype(bf16)
        few = COARSE // 4
        for ref, first, rows, bits in (
            (pair, 0, half, 0), (sib_in, BLOCK, COARSE, 1), (pair_a, 0, half, 2), (pair_b, 0, half, 3)
        ):
            base = bits * COARSE
            load_sums(ref, first, rows, sums, counts, base)
            step = rows // few
            store_means(
                three, quarter_at(index, bits), pooled(sums, few, step, base),
                pooled(counts, few, step, base), width,
            )

    return kernel


def attention_kernel(width, shard_rows, group_rows):
    far_rows = LEVELS * COARSE
    scale = HEAD_DIM**-0.5
    main_rows = far_rows + 2 * BLOCK
    key_rows = main_rows + BLOCK
    half = COARSE // 2

    def kernel(
        index, query, cot, sib, oth, sib_in, oth_in, pair_a, pair_b, three_in, shard_in, six_in,
        seven_a, seven_b, group_in,
        attended, query_grad, own_grad, sib_grad, oth_grad, low_grad, three_out,
        shard_part, six_out, seven_a_out, seven_b_out, group_out,
        keys, bias, inverse, sums, counts, score, weight, grads,
    ):
        parity, octet, half_shard, quad_group, half_group = (
            coordinate(index, 0), coordinate(index, 4), coordinate(index, 5), coordinate(index, 6), coordinate(index, 7)
        )
        packed = 2 * width

        def take(at, ref, first, rows):
            keys[pl.ds(at, rows)] = ref[pl.ds(first, rows), pl.ds(0, packed)]
            count = ref[pl.ds(first, rows), pl.ds(packed, LANES)].astype(f32)
            bias[pl.ds(at, rows)] = jnp.where(count > 0, 0.0, MASKED)
            if at < far_rows:
                inverse[pl.ds(at, rows)] = 1.0 / jnp.maximum(count, 1.0)

        def take_pooled(at):
            count = pooled(counts, COARSE, 2)
            inv = 1.0 / jnp.maximum(count, 1.0)
            keys[pl.ds(at, COARSE)] = (pooled(sums, COARSE, 2) * by_lanes(inv, packed)).astype(bf16)
            bias[pl.ds(at, COARSE)] = jnp.where(count > 0, 0.0, MASKED)
            inverse[pl.ds(at, COARSE)] = inv

        octet_at = pl.multiple_of(octet * COARSE, COARSE)
        half_shard_at = pl.multiple_of(half_shard * 2 * COARSE, 2 * COARSE)
        quad_at = pl.multiple_of(quad_group * COARSE, COARSE)
        half_group_at = pl.multiple_of(half_group * 2 * COARSE, 2 * COARSE)
        take(0, sib_in, BLOCK, COARSE)
        take(COARSE, pair_a, 0, half)
        take(COARSE + half, pair_b, 0, half)
        take(2 * COARSE, three_in, 0, COARSE)
        take(3 * COARSE, shard_in, octet_at, COARSE)
        load_sums(shard_in, half_shard_at, 2 * COARSE, sums, counts, 0)
        take_pooled(4 * COARSE)
        take(5 * COARSE, six_in, 0, COARSE)
        take(6 * COARSE, seven_a, 0, half)
        take(6 * COARSE + half, seven_b, 0, half)
        at = 7 * COARSE
        keys[pl.ds(at, COARSE)] = group_in[pl.ds(quad_at, COARSE)]
        nine = group_in[pl.ds(half_group_at, 2 * COARSE)].astype(f32)
        nine = nine.reshape(8, 2 * COARSE // 8, packed)[:, : COARSE // 8].reshape(COARSE, packed)
        keys[pl.ds(at + COARSE, COARSE)] = nine.astype(bf16)
        bias[pl.ds(at, 2 * COARSE)] = jnp.zeros((2 * COARSE, LANES), f32)
        inverse[pl.ds(at, 2 * COARSE)] = jnp.ones((2 * COARSE, LANES), f32)
        take(far_rows, sib, 0, BLOCK)
        take(far_rows + BLOCK, oth, 0, BLOCK)
        take(main_rows, sib_in, 0, BLOCK)
        take(main_rows + BLOCK, oth_in, 0, BLOCK)

        own_rows = (
            pl.ds(pl.multiple_of((1 - parity) * BLOCK, BLOCK), BLOCK),
            pl.ds(pl.multiple_of(parity * BLOCK, BLOCK), BLOCK),
        )
        nt = (((1,), (1,)), ((), ()))
        tn = (((0,), (0,)), ((), ()))
        segments = [(at, 64) for at in range(0, main_rows, 64)]
        halo_segments = [(at, 64) for at in range(0, BLOCK, 64)]

        def one_head(head):
            key_cols = pl.ds(head * HEAD_DIM, HEAD_DIM)
            value_cols = pl.ds(width + head * HEAD_DIM, HEAD_DIM)
            q = jnp.concatenate([query[r, key_cols] for r in own_rows], axis=0)
            c = jnp.concatenate([cot[r, key_cols] for r in own_rows], axis=0)

            def dots(cols, side):
                return (
                    lax.dot_general(keys[pl.ds(0, main_rows), cols], side, nt, preferred_element_type=f32),
                    lax.dot_general(
                        keys[pl.ds(main_rows, BLOCK), cols], side[:BLOCK], nt, preferred_element_type=f32
                    ),
                    lax.dot_general(
                        keys[pl.ds(main_rows + BLOCK, BLOCK), cols], side[BLOCK:], nt,
                        preferred_element_type=f32,
                    ),
                )

            main, near_sib, near_oth = dots(key_cols, q)
            score[pl.ds(0, main_rows)] = main * scale + by_lanes(bias[pl.ds(0, main_rows)], 2 * BLOCK)
            score[pl.ds(main_rows, BLOCK)] = jnp.concatenate(
                [
                    near_sib * scale + bias[pl.ds(main_rows, BLOCK)],
                    near_oth * scale + bias[pl.ds(main_rows + BLOCK, BLOCK)],
                ],
                axis=1,
            )
            main, near_sib, near_oth = dots(value_cols, c)
            grads[pl.ds(0, main_rows)] = main
            grads[pl.ds(main_rows, BLOCK)] = jnp.concatenate([near_sib, near_oth], axis=1)
            top = jnp.full((8, 2 * BLOCK), -jnp.inf, f32)
            for at in range(0, key_rows, 64):
                part = score[pl.ds(at, 64)]
                top = jnp.maximum(top, jnp.max(part.reshape(8, 8, 2 * BLOCK), axis=0))
            top = jnp.max(top, axis=0, keepdims=True)
            total = jnp.zeros((8, 2 * BLOCK), f32)
            mixed = jnp.zeros((8, 2 * BLOCK), f32)
            for at in range(0, key_rows, 64):
                e = jnp.exp(score[pl.ds(at, 64)] - top)
                score[pl.ds(at, 64)] = e
                total = total + jnp.sum(e.reshape(8, 8, 2 * BLOCK), axis=0)
                mixed = mixed + jnp.sum((e * grads[pl.ds(at, 64)]).reshape(8, 8, 2 * BLOCK), axis=0)
            total = 1.0 / jnp.sum(total, axis=0, keepdims=True)
            delta = jnp.sum(mixed, axis=0, keepdims=True) * total
            for at in range(0, key_rows, 64):
                prob = score[pl.ds(at, 64)] * total
                weight[pl.ds(at, 64), pl.ds(0, 2 * BLOCK)] = prob.astype(bf16)
                ds = prob * (grads[pl.ds(at, 64)] - delta)
                weight[pl.ds(at, 64), pl.ds(2 * BLOCK, 2 * BLOCK)] = ds.astype(bf16)

            def back(offset, cols):
                out = lax.dot_general(
                    weight[pl.ds(0, main_rows), pl.ds(offset, 2 * BLOCK)],
                    keys[pl.ds(0, main_rows), cols], tn, preferred_element_type=f32,
                )
                near = []
                for i in range(2):
                    near.append(
                        lax.dot_general(
                            weight[pl.ds(main_rows, BLOCK), pl.ds(offset + i * BLOCK, BLOCK)],
                            keys[pl.ds(main_rows + i * BLOCK, BLOCK), cols], tn,
                            preferred_element_type=f32,
                        )
                    )
                return out + jnp.concatenate(near, axis=0)

            out = back(0, value_cols)
            grad = back(2 * BLOCK, key_cols) * scale
            for i, r in enumerate(own_rows):
                attended[r, key_cols] = out[i * BLOCK : (i + 1) * BLOCK].astype(bf16)
                query_grad[r, key_cols] = grad[i * BLOCK : (i + 1) * BLOCK].astype(bf16)

            for offset, cols, side, factor in (
                (2 * BLOCK, key_cols, q, scale), (0, value_cols, c, None)
            ):
                res = jnp.dot(
                    weight[pl.ds(0, main_rows), pl.ds(offset, 2 * BLOCK)], side,
                    preferred_element_type=f32,
                )
                if factor is not None:
                    res = res * factor
                far = res[:far_rows] * inverse[...]
                own_grad[:, cols] = res[far_rows:]
                low_grad[:, cols] = far[: 2 * COARSE].astype(bf16)
                three_out[:, cols] = far[2 * COARSE : 3 * COARSE].astype(bf16)
                shard_part[:, cols] = far[3 * COARSE : 5 * COARSE].astype(bf16)
                six_out[:, cols] = far[5 * COARSE : 6 * COARSE].astype(bf16)
                seven_a_out[:, cols] = far[6 * COARSE : 6 * COARSE + half].astype(bf16)
                seven_b_out[:, cols] = far[6 * COARSE + half : 7 * COARSE].astype(bf16)
                sums[head + (0 if offset else HEADS)] = far[7 * COARSE :]
                for i, out_ref in enumerate((sib_grad, oth_grad)):
                    near = jnp.dot(
                        weight[pl.ds(main_rows, BLOCK), pl.ds(offset + i * BLOCK, BLOCK)],
                        side[i * BLOCK : (i + 1) * BLOCK], preferred_element_type=f32,
                    )
                    if factor is not None:
                        near = near * factor
                    out_ref[:, cols] = near.astype(bf16)

        for head in range(HEADS):
            one_head(head)
        group_out[...] = jnp.zeros_like(group_out)
        for tile in range(sums.shape[0]):
            cols = pl.ds(tile * LANES, LANES)
            group_out[pl.ds(quad_at, COARSE), cols] = sums[tile, pl.ds(0, COARSE)].astype(bf16)
            nine = sums[tile, pl.ds(COARSE, COARSE)].reshape(8, COARSE // 8, LANES)
            wide = jnp.concatenate([nine, jnp.zeros_like(nine)], axis=1).reshape(2 * COARSE, LANES)
            group_out[pl.ds(half_group_at, 2 * COARSE), cols] = wide.astype(bf16)

    scratch = [
        pltpu.VMEM((key_rows + BLOCK, 2 * width), bf16),
        pltpu.VMEM((key_rows + BLOCK, LANES), f32),
        pltpu.VMEM((far_rows, LANES), f32),
        pltpu.VMEM((2 * width // LANES, 2 * COARSE, LANES), f32),
        pltpu.VMEM((2 * COARSE, LANES), f32),
        pltpu.VMEM((key_rows, 2 * BLOCK), f32),
        pltpu.VMEM((key_rows, 4 * BLOCK), bf16),
        pltpu.VMEM((key_rows, 2 * BLOCK), f32),
    ]
    outs = [
        shape(2 * BLOCK, width), shape(2 * BLOCK, width), shape(2 * BLOCK, 2 * width, f32),
        shape(BLOCK, 2 * width), shape(BLOCK, 2 * width), shape(2 * COARSE, 2 * width),
        shape(COARSE, 2 * width), shape(2 * COARSE, 2 * width), shape(COARSE, 2 * width),
        shape(half, 2 * width), shape(half, 2 * width), shape(group_rows, 2 * width),
    ]
    return kernel, outs, scratch


def widen(rows, times):
    count, width = rows.shape
    return jnp.broadcast_to(rows[:, None], (count, times, width)).reshape(count * times, width)


def back_kernel(
    index, part, six, seven_a, seven_b, group, shares, three, low, sib_grad,
    out, sib_out, pair_a, pair_b, mine, acc,
):
    octet, half_shard = coordinate(index, 4), coordinate(index, 5)
    tile = six[...].astype(f32) + widen(seven_a[...].astype(f32) + seven_b[...].astype(f32), 2)
    few = COARSE // 4
    quad_at = pl.multiple_of(coordinate(index, 6) * COARSE, COARSE)
    half_at = pl.multiple_of(coordinate(index, 7) * 2 * COARSE, 2 * COARSE)
    eight = jnp.sum(group[pl.ds(quad_at, COARSE)].astype(f32).reshape(4, few, -1), axis=0)
    nine = group[pl.ds(half_at, 2 * COARSE)].astype(f32).reshape(8, few, -1)[:, : few // 2]
    nine = jnp.sum(nine, axis=0)
    share = by_lanes(shares[...], tile.shape[1])
    tile = tile + widen(eight * share[:few], 4) + widen(nine * share[few : few + few // 2], 8)
    acc[...] = widen(tile, out.shape[0] // COARSE)
    octet_at = pl.ds(pl.multiple_of(octet * COARSE, COARSE), COARSE)
    half_at = pl.ds(pl.multiple_of(half_shard * 2 * COARSE, 2 * COARSE), 2 * COARSE)
    acc[octet_at] = acc[octet_at] + part[pl.ds(0, COARSE)].astype(f32)
    acc[half_at] = acc[half_at] + widen(part[pl.ds(COARSE, COARSE)].astype(f32), 2)
    out[...] = acc[...].astype(bf16)
    half = COARSE // 2

    def quarter(bits):
        return three[pl.ds(quarter_at(index, bits), few)].astype(f32)

    sib_out[pl.ds(0, BLOCK)] = sib_grad[...]
    sib_out[pl.ds(BLOCK, COARSE)] = (low[pl.ds(0, COARSE)].astype(f32) + widen(quarter(1), 4)).astype(bf16)
    pair_a[...] = (low[pl.ds(COARSE, half)].astype(f32) + widen(quarter(2), 2)).astype(bf16)
    pair_b[...] = (low[pl.ds(COARSE + half, half)].astype(f32) + widen(quarter(3), 2)).astype(bf16)
    mine[...] = quarter(0)


def final_kernel(width):
    def kernel(
        index, mask, own, sib_back, oth_back, pair_a, pair_b, mine, shard,
        key_grad, value_grad, spread,
    ):
        parity = coordinate(index, 0)
        tokens = key_grad.shape[0]
        length = jnp.sum(mask[...], axis=1, keepdims=True)
        few = shard.shape[1]
        total = shard[0].astype(f32)
        for i in range(1, shard.shape[0]):
            total = total + shard[i].astype(f32)
        tile = widen(total, COARSE // few) + widen(mine[...], 4)
        tile = tile + widen(pair_a[...].astype(f32) + pair_b[...].astype(f32), 2)
        tile = tile + sib_back[pl.ds(BLOCK, COARSE)].astype(f32)
        spread[...] = widen(tile, tokens // COARSE)
        for i, (block, near) in enumerate(((1 - parity, sib_back), (parity, oth_back))):
            start = pl.multiple_of(block * BLOCK, BLOCK)
            live = (rows_of((BLOCK, LANES)) + start < length).astype(f32)
            grad = own[pl.ds(i * BLOCK, BLOCK)] + near[pl.ds(0, BLOCK)].astype(f32)
            grad = grad + spread[pl.ds(start, BLOCK)] * by_lanes(live, 2 * width)
            key_grad[pl.ds(start, BLOCK)] = grad[:, :width].astype(bf16)
            value_grad[pl.ds(start, BLOCK)] = grad[:, width:].astype(bf16)

    return kernel


def flip(count, bits):
    return [(i, i ^ bits) for i in range(count)]


def body(query_states, key_states, value_states, valid_mask, attended_grad):
    tokens, width = query_states.shape
    shards = lax.axis_size("shard")
    groups = lax.axis_size("grp")
    total = shards * groups
    packed = 2 * width
    row = packed + LANES
    half = COARSE // 2
    index = lax.axis_index(("grp", "shard")).astype(jnp.int32).reshape(1)
    mask = valid_mask.reshape(1, tokens)
    pairs = [(2 * i - 1, 2 * i) for i in range(1, total // 2)]
    pairs = pairs + [(high, low) for low, high in pairs]

    def on_shard(x, bits):
        return lax.ppermute(x, "shard", flip(shards, bits))

    def on_group(x, bits):
        return lax.ppermute(x, "grp", flip(groups, bits))

    few_shard = 2 * COARSE // 16
    few_group = COARSE // 4
    sib, oth, pair, gather = call(
        local_kernel(width, shards),
        [
            shape(BLOCK + COARSE, row), shape(BLOCK, row), shape(half, row),
            jax.ShapeDtypeStruct((shards, few_shard, row), bf16),
        ],
        [], index, mask, key_states, value_states, name="local", room=62,
    )
    sib_in = on_shard(sib, 1)
    pair_a = on_shard(pair, 2)
    pair_b = on_shard(pair, 3)
    oth_in = lax.ppermute(oth, ("grp", "shard"), pairs)
    shard_in = lax.all_to_all(gather, "shard", 0, 0, tiled=True).reshape(shards * few_shard, row)
    three, six, seven, wide, shares = call(
        climb_kernel(groups),
        [
            shape(COARSE, row), shape(COARSE, row), shape(half, row),
            jax.ShapeDtypeStruct((groups, few_group, packed), bf16),
            shape(few_group + few_group // 2, LANES, f32),
        ],
        [
            pltpu.VMEM((packed // LANES, shards * few_shard, LANES), f32),
            pltpu.VMEM((shards * few_shard, LANES), f32),
        ],
        index, sib_in, pair, pair_a, pair_b, shard_in, name="climb",
    )
    six_in = on_group(six, 1)
    seven_a = on_group(seven, 2)
    seven_b = on_group(seven, 3)
    three_in = on_shard(three, 4)
    group_in = lax.all_to_all(wide, "grp", 0, 0, tiled=True).reshape(groups * few_group, packed)
    kernel, outs, scratch = attention_kernel(width, shards * few_shard, groups * few_group)
    (
        attended, query_grad, own_grad, sib_grad, oth_grad, low_grad, three_out, shard_part,
        six_out, seven_a_out, seven_b_out, group_out,
    ) = call(
        kernel, outs, scratch, index, query_states, attended_grad, sib, oth, sib_in, oth_in,
        pair_a, pair_b, three_in, shard_in, six_in, seven_a, seven_b, group_in,
        flops=1_600_000_000, name="attention", room=62,
    )
    six_back = on_group(six_out, 1)
    seven_a_back = on_group(seven_a_out, 2)
    seven_b_back = on_group(seven_b_out, 3)
    three_back = on_shard(three_out, 4)
    oth_back = lax.ppermute(oth_grad, ("grp", "shard"), pairs)
    group_back = lax.all_to_all(group_out, "grp", 0, 0, tiled=True)
    oth_back, group_back = lax.optimization_barrier((oth_back, group_back))
    shard_out, sib_out, pair_a_out, pair_b_out, mine = call(
        back_kernel,
        [
            shape(shards * few_shard, packed), shape(BLOCK + COARSE, packed),
            shape(half, packed), shape(half, packed), shape(few_group, packed, f32),
        ],
        [pltpu.VMEM((shards * few_shard, packed), f32)],
        index, shard_part, six_back, seven_a_back, seven_b_back, group_back, shares, three_back,
        low_grad, sib_grad, name="back",
    )
    sib_back = on_shard(sib_out, 1)
    pair_a_back = on_shard(pair_a_out, 2)
    pair_b_back = on_shard(pair_b_out, 3)
    shard_back = lax.all_to_all(shard_out, "shard", 0, 0, tiled=True)
    key_grad, value_grad = call(
        final_kernel(width), [shape(tokens, width), shape(tokens, width)],
        [pltpu.VMEM((tokens, packed), f32)],
        index, mask, own_grad, sib_back, oth_back, pair_a_back, pair_b_back, mine,
        shard_back.reshape(shards, few_shard, packed), name="final",
    )
    return attended, query_grad, key_grad, value_grad


def solution(mesh):
    whole = P(("grp", "shard"), None)
    return jax.shard_map(
        body,
        mesh=mesh,
        in_specs=(whole, whole, whole, P(("grp", "shard")), whole),
        out_specs=(whole, whole, whole, whole),
        check_vma=False,
    )
```

```python
import jax
import jax.numpy as jnp
from jax import lax
from jax.experimental import pallas as pl
from jax.experimental.pallas import tpu as pltpu
from jax.sharding import PartitionSpec as P

HEADS = 4
HEAD_DIM = 128
BLOCK = 128
COARSE = 64
LEVELS = 9
LANES = 128
MASKED = -1e30
VMEM_BYTES = 56 * 1024 * 1024

f32 = jnp.float32
bf16 = jnp.bfloat16


def coordinate(index, item):
    device = index[0]
    shard = device & 31
    group = device >> 5
    if item == 3:
        return shard
    if item < 3:
        return shard >> item & 1
    if item < 6:
        return shard >> (item - 1) ^ 1
    return group >> (item - 4) ^ 1


def rows_of(shape):
    return lax.broadcasted_iota(jnp.int32, shape, 0)


def call(kernel, outs, scratch, index, *operands, flops=0, name=None, room=8):
    size = sum(o.size * o.dtype.itemsize for o in operands)
    size += sum(o.size * o.dtype.itemsize for o in outs)
    in_specs = [pl.BlockSpec(memory_space=pltpu.SMEM)]
    in_specs += [pl.BlockSpec(memory_space=pltpu.VMEM) for _ in operands]
    return pl.pallas_call(
        kernel,
        out_shape=outs,
        in_specs=in_specs,
        out_specs=[pl.BlockSpec(memory_space=pltpu.VMEM) for _ in outs],
        scratch_shapes=scratch,
        compiler_params=pltpu.CompilerParams(vmem_limit_bytes=room * 1024 * 1024),
        cost_estimate=pl.CostEstimate(flops=flops, bytes_accessed=size, transcendentals=0),
        name=name,
    )(index, *operands)


def shape(rows, width, dtype=bf16):
    return jax.ShapeDtypeStruct((rows, width), dtype)


def by_lanes(column, width):
    return jnp.concatenate([column] * (width // LANES), axis=1)


def local_kernel(width, peers):
    def kernel(index, mask, key, value, sib, oth, pair, gather):
        parity = coordinate(index, 0)
        tokens = key.shape[0]
        length = jnp.sum(mask[...], axis=1, keepdims=True)
        for ref, block in ((sib, 1 - parity), (oth, parity)):
            start = pl.multiple_of(block * BLOCK, BLOCK)
            ref[pl.ds(0, BLOCK), pl.ds(0, width)] = key[pl.ds(start, BLOCK)]
            ref[pl.ds(0, BLOCK), pl.ds(width, width)] = value[pl.ds(start, BLOCK)]
            place = rows_of((BLOCK, LANES)) + start
            ref[pl.ds(0, BLOCK), pl.ds(2 * width, LANES)] = (place < length).astype(f32).astype(bf16)

        def means(rows):
            group = tokens // rows
            row = rows_of((rows, tokens))
            place = lax.broadcasted_iota(jnp.int32, (rows, tokens), 1)
            member = (row * group <= place) & (place < row * group + group) & (place < length)
            member = member.astype(f32).astype(bf16)
            first = rows_of((rows, LANES)) * group
            count = jnp.clip(length - first, 0, group).astype(f32)
            inverse = by_lanes(1.0 / jnp.maximum(count, 1.0), width)
            k_sum = jnp.dot(member, key[...], preferred_element_type=f32)
            v_sum = jnp.dot(member, value[...], preferred_element_type=f32)
            return (k_sum * inverse).astype(bf16), (v_sum * inverse).astype(bf16), count.astype(bf16)

        k_mean, v_mean, count = means(COARSE)
        sib[pl.ds(BLOCK, COARSE), pl.ds(0, width)] = k_mean
        sib[pl.ds(BLOCK, COARSE), pl.ds(width, width)] = v_mean
        sib[pl.ds(BLOCK, COARSE), pl.ds(2 * width, LANES)] = count
        k_mean, v_mean, count = means(COARSE // 2)
        pair[:, pl.ds(0, width)] = k_mean
        pair[:, pl.ds(width, width)] = v_mean
        pair[:, pl.ds(2 * width, LANES)] = count
        few = gather.shape[1]
        k_mean, v_mean, count = means(few)
        for peer in range(peers):
            gather[peer, :, pl.ds(0, width)] = k_mean
            gather[peer, :, pl.ds(width, width)] = v_mean
            gather[peer, :, pl.ds(2 * width, LANES)] = count

    return kernel


def store_means(out, first, sums, count, scale_width):
    inverse = by_lanes(1.0 / jnp.maximum(count, 1.0), scale_width)
    rows = count.shape[0]
    out[pl.ds(first, rows), pl.ds(0, scale_width)] = (sums * inverse).astype(bf16)
    out[pl.ds(first, rows), pl.ds(scale_width, LANES)] = count.astype(bf16)


def load_sums(ref, first, rows, sums, counts, at):
    width = sums.shape[0] * LANES
    count = ref[pl.ds(first, rows), pl.ds(width, LANES)].astype(f32)
    counts[pl.ds(at, rows)] = count
    for tile in range(sums.shape[0]):
        mean = ref[pl.ds(first, rows), pl.ds(tile * LANES, LANES)].astype(f32)
        sums[tile, pl.ds(at, rows)] = mean * count


def pooled(ref, rows, step, base=0):
    if len(ref.shape) == 3:
        return jnp.concatenate(
            [pooled(ref.at[tile], rows, step, base) for tile in range(ref.shape[0])], axis=1
        )
    total = ref[pl.ds(base, rows, stride=step)]
    for i in range(1, step):
        total = total + ref[pl.ds(base + i, rows, stride=step)]
    return total


def quarter_at(index, flip_bits):
    few = COARSE // 4
    return pl.multiple_of(((coordinate(index, 3) & 3) ^ flip_bits) * few, few)


def climb_kernel(groups):
    def kernel(
        index, sib_in, pair, pair_a, pair_b, recv, three, six, seven, wide, shares, sums, counts
    ):
        width = sums.shape[0] * LANES
        total = recv.shape[0]
        load_sums(recv, 0, total, sums, counts, 0)
        quarter = total // COARSE
        store_means(six, 0, pooled(sums, COARSE, quarter), pooled(counts, COARSE, quarter), width)
        half = COARSE // 2
        store_means(
            seven, 0, pooled(sums, half, 2 * quarter), pooled(counts, half, 2 * quarter), width
        )
        far_half = coordinate(index, 7)
        held = wide.shape[1]
        for side, rows in ((1 - far_half, held), (far_half, held // 2)):
            count = pooled(counts, rows, total // rows)
            share = 1.0 / jnp.maximum(count, 1.0)
            mean = pooled(sums, rows, total // rows) * by_lanes(share, width)
            if rows < held:
                shares[pl.ds(held, rows)] = share
                mean = jnp.concatenate([mean, jnp.zeros_like(mean)], axis=0)
            else:
                shares[pl.ds(0, rows)] = share
            for i in range(groups // 2):
                wide[side * (groups // 2) + i] = mean.astype(bf16)
        few = COARSE // 4
        for ref, first, rows, bits in (
            (pair, 0, half, 0), (sib_in, BLOCK, COARSE, 1), (pair_a, 0, half, 2), (pair_b, 0, half, 3)
        ):
            base = bits * COARSE
            load_sums(ref, first, rows, sums, counts, base)
            step = rows // few
            store_means(
                three, quarter_at(index, bits), pooled(sums, few, step, base),
                pooled(counts, few, step, base), width,
            )

    return kernel


def attention_kernel(width, shard_rows, group_rows):
    far_rows = LEVELS * COARSE
    scale = HEAD_DIM**-0.5
    main_rows = far_rows + 2 * BLOCK
    key_rows = main_rows + BLOCK
    half = COARSE // 2

    def kernel(
        index, query, cot, sib, oth, sib_in, oth_in, pair_a, pair_b, three_in, shard_in, six_in,
        seven_a, seven_b, group_in,
        attended, query_grad, own_grad, sib_grad, oth_grad, low_grad, three_out,
        shard_part, six_out, seven_a_out, seven_b_out, group_out,
        keys, bias, inverse, sums, counts, score, weight, grads,
    ):
        parity, octet, half_shard, quad_group, half_group = (
            coordinate(index, 0), coordinate(index, 4), coordinate(index, 5), coordinate(index, 6), coordinate(index, 7)
        )
        packed = 2 * width

        def take(at, ref, first, rows):
            keys[pl.ds(at, rows)] = ref[pl.ds(first, rows), pl.ds(0, packed)]
            count = ref[pl.ds(first, rows), pl.ds(packed, LANES)].astype(f32)
            bias[pl.ds(at, rows)] = jnp.where(count > 0, 0.0, MASKED)
            if at < far_rows:
                inverse[pl.ds(at, rows)] = 1.0 / jnp.maximum(count, 1.0)

        def take_pooled(at):
            count = pooled(counts, COARSE, 2)
            inv = 1.0 / jnp.maximum(count, 1.0)
            keys[pl.ds(at, COARSE)] = (pooled(sums, COARSE, 2) * by_lanes(inv, packed)).astype(bf16)
            bias[pl.ds(at, COARSE)] = jnp.where(count > 0, 0.0, MASKED)
            inverse[pl.ds(at, COARSE)] = inv

        octet_at = pl.multiple_of(octet * COARSE, COARSE)
        half_shard_at = pl.multiple_of(half_shard * 2 * COARSE, 2 * COARSE)
        quad_at = pl.multiple_of(quad_group * COARSE, COARSE)
        half_group_at = pl.multiple_of(half_group * 2 * COARSE, 2 * COARSE)
        take(0, sib_in, BLOCK, COARSE)
        take(COARSE, pair_a, 0, half)
        take(COARSE + half, pair_b, 0, half)
        take(2 * COARSE, three_in, 0, COARSE)
        take(3 * COARSE, shard_in, octet_at, COARSE)
        load_sums(shard_in, half_shard_at, 2 * COARSE, sums, counts, 0)
        take_pooled(4 * COARSE)
        take(5 * COARSE, six_in, 0, COARSE)
        take(6 * COARSE, seven_a, 0, half)
        take(6 * COARSE + half, seven_b, 0, half)
        at = 7 * COARSE
        keys[pl.ds(at, COARSE)] = group_in[pl.ds(quad_at, COARSE)]
        nine = group_in[pl.ds(half_group_at, 2 * COARSE)].astype(f32)
        nine = nine.reshape(8, 2 * COARSE // 8, packed)[:, : COARSE // 8].reshape(COARSE, packed)
        keys[pl.ds(at + COARSE, COARSE)] = nine.astype(bf16)
        bias[pl.ds(at, 2 * COARSE)] = jnp.zeros((2 * COARSE, LANES), f32)
        inverse[pl.ds(at, 2 * COARSE)] = jnp.ones((2 * COARSE, LANES), f32)
        take(far_rows, sib, 0, BLOCK)
        take(far_rows + BLOCK, oth, 0, BLOCK)
        take(main_rows, sib_in, 0, BLOCK)
        take(main_rows + BLOCK, oth_in, 0, BLOCK)

        own_rows = (
            pl.ds(pl.multiple_of((1 - parity) * BLOCK, BLOCK), BLOCK),
            pl.ds(pl.multiple_of(parity * BLOCK, BLOCK), BLOCK),
        )
        nt = (((1,), (1,)), ((), ()))
        tn = (((0,), (0,)), ((), ()))
        segments = [(at, 64) for at in range(0, main_rows, 64)]
        halo_segments = [(at, 64) for at in range(0, BLOCK, 64)]

        def one_head(head):
            key_cols = pl.ds(head * HEAD_DIM, HEAD_DIM)
            value_cols = pl.ds(width + head * HEAD_DIM, HEAD_DIM)
            q = jnp.concatenate([query[r, key_cols] for r in own_rows], axis=0)
            c = jnp.concatenate([cot[r, key_cols] for r in own_rows], axis=0)

            def dots(cols, side):
                return (
                    lax.dot_general(keys[pl.ds(0, main_rows), cols], side, nt, preferred_element_type=f32),
                    lax.dot_general(
                        keys[pl.ds(main_rows, BLOCK), cols], side[:BLOCK], nt, preferred_element_type=f32
                    ),
                    lax.dot_general(
                        keys[pl.ds(main_rows + BLOCK, BLOCK), cols], side[BLOCK:], nt,
                        preferred_element_type=f32,
                    ),
                )

            main, near_sib, near_oth = dots(key_cols, q)
            score[pl.ds(0, main_rows)] = main * scale + by_lanes(bias[pl.ds(0, main_rows)], 2 * BLOCK)
            score[pl.ds(main_rows, BLOCK)] = jnp.concatenate(
                [
                    near_sib * scale + bias[pl.ds(main_rows, BLOCK)],
                    near_oth * scale + bias[pl.ds(main_rows + BLOCK, BLOCK)],
                ],
                axis=1,
            )
            main, near_sib, near_oth = dots(value_cols, c)
            grads[pl.ds(0, main_rows)] = main
            grads[pl.ds(main_rows, BLOCK)] = jnp.concatenate([near_sib, near_oth], axis=1)
            top = jnp.full((8, 2 * BLOCK), -jnp.inf, f32)
            for at in range(0, key_rows, 64):
                part = score[pl.ds(at, 64)]
                top = jnp.maximum(top, jnp.max(part.reshape(8, 8, 2 * BLOCK), axis=0))
            top = jnp.max(top, axis=0, keepdims=True)
            total = jnp.zeros((8, 2 * BLOCK), f32)
            mixed = jnp.zeros((8, 2 * BLOCK), f32)
            for at in range(0, key_rows, 64):
                e = jnp.exp(score[pl.ds(at, 64)] - top)
                score[pl.ds(at, 64)] = e
                total = total + jnp.sum(e.reshape(8, 8, 2 * BLOCK), axis=0)
                mixed = mixed + jnp.sum((e * grads[pl.ds(at, 64)]).reshape(8, 8, 2 * BLOCK), axis=0)
            total = 1.0 / jnp.sum(total, axis=0, keepdims=True)
            delta = jnp.sum(mixed, axis=0, keepdims=True) * total
            for at in range(0, key_rows, 64):
                prob = score[pl.ds(at, 64)] * total
                weight[pl.ds(at, 64), pl.ds(0, 2 * BLOCK)] = prob.astype(bf16)
                ds = prob * (grads[pl.ds(at, 64)] - delta)
                weight[pl.ds(at, 64), pl.ds(2 * BLOCK, 2 * BLOCK)] = ds.astype(bf16)

            def back(offset, cols):
                out = lax.dot_general(
                    weight[pl.ds(0, main_rows), pl.ds(offset, 2 * BLOCK)],
                    keys[pl.ds(0, main_rows), cols], tn, preferred_element_type=f32,
                )
                near = []
                for i in range(2):
                    near.append(
                        lax.dot_general(
                            weight[pl.ds(main_rows, BLOCK), pl.ds(offset + i * BLOCK, BLOCK)],
                            keys[pl.ds(main_rows + i * BLOCK, BLOCK), cols], tn,
                            preferred_element_type=f32,
                        )
                    )
                return out + jnp.concatenate(near, axis=0)

            out = back(0, value_cols)
            grad = back(2 * BLOCK, key_cols) * scale
            for i, r in enumerate(own_rows):
                attended[r, key_cols] = out[i * BLOCK : (i + 1) * BLOCK].astype(bf16)
                query_grad[r, key_cols] = grad[i * BLOCK : (i + 1) * BLOCK].astype(bf16)

            for offset, cols, side, factor in (
                (2 * BLOCK, key_cols, q, scale), (0, value_cols, c, None)
            ):
                res = jnp.dot(
                    weight[pl.ds(0, main_rows), pl.ds(offset, 2 * BLOCK)], side,
                    preferred_element_type=f32,
                )
                if factor is not None:
                    res = res * factor
                far = res[:far_rows] * inverse[...]
                own_grad[:, cols] = res[far_rows:].astype(bf16)
                low_grad[:, cols] = far[: 2 * COARSE].astype(bf16)
                three_out[:, cols] = far[2 * COARSE : 3 * COARSE].astype(bf16)
                shard_part[:, cols] = far[3 * COARSE : 5 * COARSE].astype(bf16)
                six_out[:, cols] = far[5 * COARSE : 6 * COARSE].astype(bf16)
                seven_a_out[:, cols] = far[6 * COARSE : 6 * COARSE + half].astype(bf16)
                seven_b_out[:, cols] = far[6 * COARSE + half : 7 * COARSE].astype(bf16)
                sums[head + (0 if offset else HEADS)] = far[7 * COARSE :]
                for i, out_ref in enumerate((sib_grad, oth_grad)):
                    near = jnp.dot(
                        weight[pl.ds(main_rows, BLOCK), pl.ds(offset + i * BLOCK, BLOCK)],
                        side[i * BLOCK : (i + 1) * BLOCK], preferred_element_type=f32,
                    )
                    if factor is not None:
                        near = near * factor
                    out_ref[:, cols] = near.astype(bf16)

        for head in range(HEADS):
            one_head(head)
        group_out[...] = jnp.zeros_like(group_out)
        for tile in range(sums.shape[0]):
            cols = pl.ds(tile * LANES, LANES)
            group_out[pl.ds(quad_at, COARSE), cols] = sums[tile, pl.ds(0, COARSE)].astype(bf16)
            nine = sums[tile, pl.ds(COARSE, COARSE)].reshape(8, COARSE // 8, LANES)
            wide = jnp.concatenate([nine, jnp.zeros_like(nine)], axis=1).reshape(2 * COARSE, LANES)
            group_out[pl.ds(half_group_at, 2 * COARSE), cols] = wide.astype(bf16)

    scratch = [
        pltpu.VMEM((key_rows + BLOCK, 2 * width), bf16),
        pltpu.VMEM((key_rows + BLOCK, LANES), f32),
        pltpu.VMEM((far_rows, LANES), f32),
        pltpu.VMEM((2 * width // LANES, 2 * COARSE, LANES), f32),
        pltpu.VMEM((2 * COARSE, LANES), f32),
        pltpu.VMEM((key_rows, 2 * BLOCK), f32),
        pltpu.VMEM((key_rows, 4 * BLOCK), bf16),
        pltpu.VMEM((key_rows, 2 * BLOCK), f32),
    ]
    outs = [
        shape(2 * BLOCK, width), shape(2 * BLOCK, width), shape(2 * BLOCK, 2 * width),
        shape(BLOCK, 2 * width), shape(BLOCK, 2 * width), shape(2 * COARSE, 2 * width),
        shape(COARSE, 2 * width), shape(2 * COARSE, 2 * width), shape(COARSE, 2 * width),
        shape(half, 2 * width), shape(half, 2 * width), shape(group_rows, 2 * width),
    ]
    return kernel, outs, scratch


def widen(rows, times):
    count, width = rows.shape
    return jnp.broadcast_to(rows[:, None], (count, times, width)).reshape(count * times, width)


def back_kernel(
    index, part, six, seven_a, seven_b, group, shares, three, low, sib_grad,
    out, sib_out, pair_a, pair_b, mine, acc,
):
    octet, half_shard = coordinate(index, 4), coordinate(index, 5)
    tile = six[...].astype(f32) + widen(seven_a[...].astype(f32) + seven_b[...].astype(f32), 2)
    few = COARSE // 4
    quad_at = pl.multiple_of(coordinate(index, 6) * COARSE, COARSE)
    half_at = pl.multiple_of(coordinate(index, 7) * 2 * COARSE, 2 * COARSE)
    eight = jnp.sum(group[pl.ds(quad_at, COARSE)].astype(f32).reshape(4, few, -1), axis=0)
    nine = group[pl.ds(half_at, 2 * COARSE)].astype(f32).reshape(8, few, -1)[:, : few // 2]
    nine = jnp.sum(nine, axis=0)
    share = by_lanes(shares[...], tile.shape[1])
    tile = tile + widen(eight * share[:few], 4) + widen(nine * share[few : few + few // 2], 8)
    acc[...] = widen(tile, out.shape[0] // COARSE)
    octet_at = pl.ds(pl.multiple_of(octet * COARSE, COARSE), COARSE)
    half_at = pl.ds(pl.multiple_of(half_shard * 2 * COARSE, 2 * COARSE), 2 * COARSE)
    acc[octet_at] = acc[octet_at] + part[pl.ds(0, COARSE)].astype(f32)
    acc[half_at] = acc[half_at] + widen(part[pl.ds(COARSE, COARSE)].astype(f32), 2)
    out[...] = acc[...].astype(bf16)
    half = COARSE // 2

    def quarter(bits):
        return three[pl.ds(quarter_at(index, bits), few)].astype(f32)

    sib_out[pl.ds(0, BLOCK)] = sib_grad[...]
    sib_out[pl.ds(BLOCK, COARSE)] = (low[pl.ds(0, COARSE)].astype(f32) + widen(quarter(1), 4)).astype(bf16)
    pair_a[...] = (low[pl.ds(COARSE, half)].astype(f32) + widen(quarter(2), 2)).astype(bf16)
    pair_b[...] = (low[pl.ds(COARSE + half, half)].astype(f32) + widen(quarter(3), 2)).astype(bf16)
    mine[...] = quarter(0)


def final_kernel(width):
    def kernel(
        index, mask, own, sib_back, oth_back, pair_a, pair_b, mine, shard,
        key_grad, value_grad, spread,
    ):
        parity = coordinate(index, 0)
        tokens = key_grad.shape[0]
        length = jnp.sum(mask[...], axis=1, keepdims=True)
        few = shard.shape[1]
        total = shard[0].astype(f32)
        for i in range(1, shard.shape[0]):
            total = total + shard[i].astype(f32)
        tile = widen(total, COARSE // few) + widen(mine[...], 4)
        tile = tile + widen(pair_a[...].astype(f32) + pair_b[...].astype(f32), 2)
        tile = tile + sib_back[pl.ds(BLOCK, COARSE)].astype(f32)
        spread[...] = widen(tile, tokens // COARSE)
        for i, (block, near) in enumerate(((1 - parity, sib_back), (parity, oth_back))):
            start = pl.multiple_of(block * BLOCK, BLOCK)
            live = (rows_of((BLOCK, LANES)) + start < length).astype(f32)
            grad = own[pl.ds(i * BLOCK, BLOCK)].astype(f32) + near[pl.ds(0, BLOCK)].astype(f32)
            grad = grad + spread[pl.ds(start, BLOCK)] * by_lanes(live, 2 * width)
            key_grad[pl.ds(start, BLOCK)] = grad[:, :width].astype(bf16)
            value_grad[pl.ds(start, BLOCK)] = grad[:, width:].astype(bf16)

    return kernel


def flip(count, bits):
    return [(i, i ^ bits) for i in range(count)]


def body(query_states, key_states, value_states, valid_mask, attended_grad):
    tokens, width = query_states.shape
    shards = lax.axis_size("shard")
    groups = lax.axis_size("grp")
    total = shards * groups
    packed = 2 * width
    row = packed + LANES
    half = COARSE // 2
    index = lax.axis_index(("grp", "shard")).astype(jnp.int32).reshape(1)
    mask = valid_mask.reshape(1, tokens)
    pairs = [(2 * i - 1, 2 * i) for i in range(1, total // 2)]
    pairs = pairs + [(high, low) for low, high in pairs]

    def on_shard(x, bits):
        return lax.ppermute(x, "shard", flip(shards, bits))

    def on_group(x, bits):
        return lax.ppermute(x, "grp", flip(groups, bits))

    few_shard = 2 * COARSE // 16
    few_group = COARSE // 4
    sib, oth, pair, gather = call(
        local_kernel(width, shards),
        [
            shape(BLOCK + COARSE, row), shape(BLOCK, row), shape(half, row),
            jax.ShapeDtypeStruct((shards, few_shard, row), bf16),
        ],
        [], index, mask, key_states, value_states, name="local", room=62,
    )
    sib_in = on_shard(sib, 1)
    pair_a = on_shard(pair, 2)
    pair_b = on_shard(pair, 3)
    oth_in = lax.ppermute(oth, ("grp", "shard"), pairs)
    shard_in = lax.all_to_all(gather, "shard", 0, 0, tiled=True).reshape(shards * few_shard, row)
    three, six, seven, wide, shares = call(
        climb_kernel(groups),
        [
            shape(COARSE, row), shape(COARSE, row), shape(half, row),
            jax.ShapeDtypeStruct((groups, few_group, packed), bf16),
            shape(few_group + few_group // 2, LANES, f32),
        ],
        [
            pltpu.VMEM((packed // LANES, shards * few_shard, LANES), f32),
            pltpu.VMEM((shards * few_shard, LANES), f32),
        ],
        index, sib_in, pair, pair_a, pair_b, shard_in, name="climb",
    )
    six_in = on_group(six, 1)
    seven_a = on_group(seven, 2)
    seven_b = on_group(seven, 3)
    three_in = on_shard(three, 4)
    group_in = lax.all_to_all(wide, "grp", 0, 0, tiled=True).reshape(groups * few_group, packed)
    kernel, outs, scratch = attention_kernel(width, shards * few_shard, groups * few_group)
    (
        attended, query_grad, own_grad, sib_grad, oth_grad, low_grad, three_out, shard_part,
        six_out, seven_a_out, seven_b_out, group_out,
    ) = call(
        kernel, outs, scratch, index, query_states, attended_grad, sib, oth, sib_in, oth_in,
        pair_a, pair_b, three_in, shard_in, six_in, seven_a, seven_b, group_in,
        flops=1_600_000_000, name="attention", room=62,
    )
    six_back = on_group(six_out, 1)
    seven_a_back = on_group(seven_a_out, 2)
    seven_b_back = on_group(seven_b_out, 3)
    three_back = on_shard(three_out, 4)
    oth_back = lax.ppermute(oth_grad, ("grp", "shard"), pairs)
    group_back = lax.all_to_all(group_out, "grp", 0, 0, tiled=True)
    oth_back, group_back = lax.optimization_barrier((oth_back, group_back))
    shard_out, sib_out, pair_a_out, pair_b_out, mine = call(
        back_kernel,
        [
            shape(shards * few_shard, packed), shape(BLOCK + COARSE, packed),
            shape(half, packed), shape(half, packed), shape(few_group, packed, f32),
        ],
        [pltpu.VMEM((shards * few_shard, packed), f32)],
        index, shard_part, six_back, seven_a_back, seven_b_back, group_back, shares, three_back,
        low_grad, sib_grad, name="back",
    )
    sib_back = on_shard(sib_out, 1)
    pair_a_back = on_shard(pair_a_out, 2)
    pair_b_back = on_shard(pair_b_out, 3)
    shard_back = lax.all_to_all(shard_out, "shard", 0, 0, tiled=True)
    key_grad, value_grad = call(
        final_kernel(width), [shape(tokens, width), shape(tokens, width)],
        [pltpu.VMEM((tokens, packed), f32)],
        index, mask, own_grad, sib_back, oth_back, pair_a_back, pair_b_back, mine,
        shard_back.reshape(shards, few_shard, packed), name="final",
    )
    return attended, query_grad, key_grad, value_grad


def solution(mesh):
    whole = P(("grp", "shard"), None)
    return jax.shard_map(
        body,
        mesh=mesh,
        in_specs=(whole, whole, whole, P(("grp", "shard")), whole),
        out_specs=(whole, whole, whole, whole),
        check_vma=False,
    )
```
